512 devices in a mesh: grp: 64 (over z, x), own: 8 (over y, core).
Axes of the slice: x: 4, y: 4, z: 16, core: 2. Of those that a mesh axis runs over, the one named last changes fastest.
Arguments:
- excitation: bfloat16 [4, 8192, 256], P(None, ('grp', 'own')), may hold values from -6 to 6
- cur_hist: bfloat16 [4, 8192, 256], P(None, ('grp', 'own')), may hold values from -6 to 6
- ret_hist: bfloat16 [4, 8192, 256], P(None, ('grp', 'own')), may hold values from -6 to 6
- pole_state: float32 [16, 8192, 256], P(None, ('grp', 'own')), may hold values from -12 to 12
- self_inverse: bfloat16 [8192, 256, 256], P(('grp', 'own')), may hold values from -0.375 to 0.375
- near_mats: bfloat16 [2, 256, 256], replicated, may hold values from -0.09375 to 0.09375
- far_mats: bfloat16 [16, 256, 256], replicated, may hold values from -0.0234375 to 0.0234375
- poles: float32 [16], replicated, may hold values from 0.3 to 0.97
- residues: float32 [16], replicated, may hold values from -0.3 to 0.3
- near_src: int32 [2, 8192, 2], P(None, ('grp', 'own')), may hold values from 0 to 15
- near_delay: int32 [2, 8192, 2], P(None, ('grp', 'own')), may hold values from 1 to 4
- far_dest: int32 [8192, 4], P(('grp', 'own')), may hold values from 0 to 63, all different within a row; in each aligned block of 16 rows (0 to 15, 16 to 31, ...) at most 2 rows name the same one
- far_delay: int32 [8192, 4], P(('grp', 'own')), may hold values from 1 to 4
- far_reader: int32 [64, 64, 8, 2, 16], P('grp', None, 'own'), may hold values from 0 to 127
Outputs:
- currents: bfloat16 [4, 8192, 256], P(None, ('grp', 'own'))
- pole_final: float32 [16, 8192, 256], P(None, ('grp', 'own'))
The draws below stay inside these ranges and needn't reach their ends.
Inputs may be any that keep to these rules, and one draw needn't show every extreme that they name: `far_dest`: each source tile names 4 different groups; among the tiles of one aligned block of 16 tiles no group is named by more than 2 tiles.
All inputs are finite; a program needn't handle non-finite values.
Results may differ from the reference program's by a relative error of at most 0.018.
Values may be sent and summed in bfloat16 or wider, within the bound.
No kernel may reach another device: no remote copies, remote signals or barrier semaphores. Data moves between devices by JAX's collectives and lax.ppermute only.
A program may use at most 64 MiB of HBM per device.

```python
import math
import jax
import jax.numpy as jnp
import numpy as np
from jax import lax

B = 256
P_SIZE = 16
KT = 16
NT = 2
NEAR_K = 2
FAR_S = 4
HIST = 4
STEPS = 4
TILES_DEV = 16
NGROUPS = 64
OWNERS = 8
TILES_GRP = 128
TILES = 8192
NBLOCKS = 512
CAP = 2


def touch_ends(values, rng, least, high):
    longest = values.shape.index(max(values.shape))
    spots = []
    for shift in (0, 1):
        where = [jax.random.randint(jax.random.fold_in(rng, axis), (), 0, length) for axis, length in enumerate(values.shape)]
        where[longest] = (where[longest] + shift) % values.shape[longest]
        spots.append(tuple(where))
    return values.at[spots[0]].set(least).at[spots[1]].set(high)


def block_levels(key, shape, pieces, low, top_value):
    def one(axis_at, parts):
        draws = jax.random.uniform(jax.random.fold_in(jax.random.fold_in(key, 6), axis_at), (parts,), jnp.float32, low / len(pieces), top_value / len(pieces))
        return jnp.repeat(jnp.exp(draws), shape[axis_at] // parts).reshape((-1,) + (1,) * (len(shape) - axis_at - 1))

    factor_of = one(*pieces[0])
    for cut in pieces[1:]:
        factor_of = factor_of * one(*cut)
    return factor_of


def assign_block(stream_key, own, number, rows, amount, top, limit, skew):
    order = jax.random.permutation(stream_key, amount)
    heavy_load, usual = load_shares(amount, rows * top, limit, skew, True), load_shares(amount, rows * top, limit, skew, False)
    places = jnp.arange(amount)

    def named(tallies, rotation):
        used = int((tallies > 0).sum())
        fixed = max(1, used // 4)
        shifted = fixed + (places - fixed + rotation * (used - fixed)) % max(1, amount - fixed)
        return jnp.zeros((amount,), jnp.int32).at[order[jnp.where(places < fixed, places, shifted)]].set(jnp.asarray(tallies, jnp.int32))

    tallies = jnp.where(number % 4 == 0, named(heavy_load, number // 4), named(usual, number - number // 4 - 1))
    mixed = jax.random.permutation(jax.random.fold_in(own, 3), amount)
    source_of, taker = mixed[0:amount // 2 * 2:2], mixed[1:amount // 2 * 2:2]
    margin = jnp.minimum(tallies[source_of] - 1, limit - tallies[taker]) // 2
    margin = jnp.where((source_of == order[0]) | (taker == order[0]) | (tallies[taker] == 0), 0, jnp.maximum(margin, 0))
    shifted = jax.random.randint(jax.random.fold_in(own, 4), (amount // 2,), 0, 1 << 20) % (margin + 1)
    tallies = tallies.at[source_of].add(-shifted).at[taker].add(shifted)
    members = jnp.searchsorted(jnp.cumsum(tallies), jnp.arange(rows * top), side="right").astype(jnp.int32)
    listing = members.reshape(top, rows).T
    listing = listing[jax.random.permutation(jax.random.fold_in(own, 1), rows)]
    rotation = jax.random.randint(jax.random.fold_in(own, 2), (rows, 1), 0, top)
    return jnp.take_along_axis(listing, (jnp.arange(top)[None, :] + rotation) % top, axis=1)


def load_shares(number_of, total, bound, lean, full):
    weights = [(1 << 20) // math.isqrt(rank ** lean) + 1 for rank in range(1, number_of + 1)]
    largest = bound if full else min(bound, max(-(-total // number_of), total * weights[0] // sum(weights)))
    least = 1 if total - largest >= number_of - 1 else 0
    given, surplus = [largest] + [least] * (number_of - 1), total - largest - least * (number_of - 1)
    while surplus > 0:
        candidates = [i for i in range(1, number_of) if given[i] < largest] or [i for i in range(1, number_of) if given[i] < bound]
        mass, budget = sum([weights[i] for i in candidates]), surplus
        for i in candidates:
            addition = min(bound - given[i], max(1, budget * weights[i] // mass), surplus)
            given[i] = given[i] + addition
            surplus = surplus - addition
    return np.array(given)


def scatter_about(stream_key, dims, scale, most, cuts=(), held_as=jnp.bfloat16):
    result = scale * jax.random.normal(stream_key, dims, jnp.float32)
    if cuts:
        result = result * block_levels(stream_key, dims, cuts, -0.22, 0.18)
    return jnp.clip(result, -most, most).astype(held_as)


def setup_inputs(seed: int = 0) -> dict:
    streams_of = jax.random.split(jax.random.key(seed), 15)
    excitation = scatter_about(streams_of[0], (STEPS, TILES, B), 1.0, 6.0, ((1, 512),))
    cur_hist = scatter_about(streams_of[1], (HIST, TILES, B), 1.0, 6.0, ((1, 512),))
    ret_hist = scatter_about(streams_of[2], (HIST, TILES, B), 1.0, 6.0, ((1, 512),))
    pole_state = scatter_about(streams_of[3], (P_SIZE, TILES, B), 2.0, 12.0, ((1, 512),), jnp.float32)
    self_inverse = scatter_about(streams_of[4], (TILES, B, B), B ** -0.5, 0.375, ((0, 512),))
    near_mats = scatter_about(streams_of[5], (NT, B, B), (4 * B * NT * NEAR_K) ** -0.5, 0.09375)
    far_mats = scatter_about(streams_of[6], (KT, B, B), (4 * B * FAR_S * KT) ** -0.5, 0.0234375)
    poles = jnp.clip(jnp.exp(jax.random.uniform(streams_of[7], (P_SIZE,), jnp.float32, math.log(0.3), math.log(0.97))), 0.3, 0.97)
    residues = jnp.clip(jax.random.uniform(streams_of[8], (P_SIZE,), jnp.float32, -0.3, 0.3), -0.3, 0.3)
    near_src = touch_ends(jax.random.randint(streams_of[9], (NT, TILES, NEAR_K), 0, TILES_DEV), jax.random.fold_in(streams_of[9], 1), 0, TILES_DEV - 1).astype(jnp.int32)
    near_delay = touch_ends(jax.random.randint(streams_of[10], (NT, TILES, NEAR_K), 1, HIST + 1), jax.random.fold_in(streams_of[10], 1), 1, HIST).astype(jnp.int32)
    far_dest_keys = jax.random.split(jax.random.fold_in(streams_of[11], 1), TILES // TILES_DEV)
    far_dest_turns = jax.random.permutation(jax.random.fold_in(streams_of[11], 3), TILES // TILES_DEV)
    far_dest = jax.vmap(lambda own, number: assign_block(jax.random.fold_in(streams_of[11], 2), own, number, TILES_DEV, NGROUPS, FAR_S, CAP, 2))(far_dest_keys, far_dest_turns).reshape((TILES, FAR_S))
    far_delay = touch_ends(jax.random.randint(streams_of[12], (TILES, FAR_S), 1, HIST + 1), jax.random.fold_in(streams_of[12], 1), 1, HIST).astype(jnp.int32)
    far_reader = touch_ends(jax.random.randint(streams_of[13], (NGROUPS, NGROUPS, OWNERS, CAP, KT), 0, TILES_GRP), jax.random.fold_in(streams_of[13], 1), 0, TILES_GRP - 1).astype(jnp.int32)
    return dict(excitation=excitation, cur_hist=cur_hist, ret_hist=ret_hist, pole_state=pole_state, self_inverse=self_inverse, near_mats=near_mats, far_mats=far_mats, poles=poles, residues=residues, near_src=near_src, near_delay=near_delay, far_dest=far_dest, far_delay=far_delay, far_reader=far_reader)


def near_part(history_cur, near_src, near_delay, near_mats):
    block_base = (jnp.arange(TILES, dtype=jnp.int32) // TILES_DEV) * TILES_DEV
    near_rows = block_base[None, :, None] + near_src
    gathered = history_cur[near_delay - 1, near_rows]
    return jnp.einsum('ktmb,kab->ta', gathered.astype(jnp.float32), near_mats.astype(jnp.float32))


def far_part(history_ret, far_dest, far_delay, far_reader, far_mats):
    tile_ids = jnp.arange(TILES, dtype=jnp.int32)
    blocks = history_ret[far_delay - 1, tile_ids[:, None]]
    dest_groups = far_dest.reshape(NBLOCKS, TILES_DEV, FAR_S)
    named_by = (dest_groups[..., None] == jnp.arange(NGROUPS, dtype=jnp.int32)).astype(jnp.int32)
    per_tile = named_by.sum(2)
    before = jnp.cumsum(per_tile, axis=1) - per_tile
    slot_rank = jnp.take_along_axis(before, dest_groups, axis=2)
    block_index = jnp.broadcast_to(jnp.arange(NBLOCKS, dtype=jnp.int32)[:, None, None], dest_groups.shape)
    outgoing = jnp.zeros((NBLOCKS, NGROUPS, CAP, B), jnp.bfloat16)
    outgoing = outgoing.at[block_index, dest_groups, slot_rank].set(blocks.reshape(NBLOCKS, TILES_DEV, FAR_S, B))
    readers = far_reader.reshape(NGROUPS, NBLOCKS, CAP, KT)

    def one_group(pair):
        incoming, chosen = pair
        far_terms = jnp.einsum('scb,kab->scka', incoming.astype(jnp.float32), far_mats.astype(jnp.float32))
        far_terms = lax.optimization_barrier(far_terms.astype(jnp.bfloat16)).astype(jnp.float32)
        reader_hits = (chosen[..., None] == jnp.arange(TILES_GRP, dtype=jnp.int32)).astype(jnp.float32)
        return jnp.einsum('scka,sckq->qa', far_terms, reader_hits)

    far_field = lax.map(one_group, (jnp.swapaxes(outgoing, 0, 1), readers))
    return far_field.reshape(TILES, B)


def solve_blocks(self_inverse, right_side):
    matrices = self_inverse.reshape(NBLOCKS, TILES_DEV, B, B)
    vectors = right_side.reshape(NBLOCKS, TILES_DEV, B)

    def one_block(pair):
        return jnp.einsum('tab,tb->ta', pair[0].astype(jnp.float32), pair[1].astype(jnp.float32))

    return lax.map(one_block, (matrices, vectors)).reshape(TILES, B)


def reference(excitation, cur_hist, ret_hist, pole_state, self_inverse, near_mats, far_mats, poles, residues, near_src, near_delay, far_dest, far_delay, far_reader):
    history_cur = cur_hist
    history_ret = ret_hist
    pole_now = pole_state
    outputs = []
    for time_step in range(STEPS):
        near_field = near_part(history_cur, near_src, near_delay, near_mats)
        far_field = far_part(history_ret, far_dest, far_delay, far_reader, far_mats)
        right_side = (excitation[time_step].astype(jnp.float32) - near_field - far_field).astype(jnp.bfloat16)
        right_side = lax.optimization_barrier(right_side)
        current_now = solve_blocks(self_inverse, right_side).astype(jnp.bfloat16)
        current_now = lax.optimization_barrier(current_now)
        outputs.append(current_now)
        current_wide = current_now.astype(jnp.float32)
        pole_now = poles[:, None, None] * pole_now + current_wide[None]
        retarded_now = (current_wide + jnp.einsum('p,ptb->tb', residues, pole_now)).astype(jnp.bfloat16)
        history_cur = jnp.concatenate([current_now[None], history_cur[:-1]], axis=0)
        history_ret = jnp.concatenate([retarded_now[None], history_ret[:-1]], axis=0)
    return jnp.stack(outputs), pole_now
```

```python
import jax
import jax.numpy as jnp
from jax import lax
from jax.sharding import PartitionSpec as P

STEPS = 4
HIST = 4
F32 = jnp.float32
BF16 = jnp.bfloat16


def body(
    excitation,
    cur_hist,
    ret_hist,
    pole_state,
    self_inverse,
    near_mats,
    far_mats,
    poles,
    residues,
    near_src,
    near_delay,
    far_dest,
    far_delay,
    far_reader,
):
    groups = far_reader.shape[1]
    cap = far_reader.shape[3]
    classes = far_reader.shape[4]
    tiles = excitation.shape[1]
    width = excitation.shape[2]
    owners = lax.axis_size("own")
    group_tiles = tiles * owners
    slots = groups * cap

    named_by = far_dest[:, :, None] == jnp.arange(groups, dtype=jnp.int32)
    named = named_by.any(1)
    named_int = named.astype(jnp.int32)
    rank = jnp.cumsum(named_int, axis=0) - named_int
    delay_of = jnp.sum(jnp.where(named_by, far_delay[:, :, None], 0), axis=1)
    send_pick = (
        named.T[:, None, None, :]
        & (rank.T[:, None, None, :] == jnp.arange(cap, dtype=jnp.int32)[None, :, None, None])
        & (
            delay_of.T[:, None, None, :]
            == jnp.arange(1, HIST + 1, dtype=jnp.int32)[None, None, :, None]
        )
    )
    send_pick = send_pick.reshape(slots, HIST * tiles).astype(BF16)

    readers = far_reader.reshape(slots, classes)
    reader_hits = (
        readers.T[None, :, :] == jnp.arange(group_tiles, dtype=jnp.int32)[:, None, None]
    ).astype(BF16)
    reader_hits = reader_hits.reshape(group_tiles, classes * slots)

    near_row = (near_delay - 1) * tiles + near_src
    near_pick = (
        near_row[..., None] == jnp.arange(HIST * tiles, dtype=jnp.int32)
    ).astype(BF16)
    near_pick = near_pick.transpose(0, 2, 1, 3)

    power = [jnp.ones_like(poles)]
    for _ in range(STEPS):
        power.append(power[-1] * poles)
    tail = [
        jnp.sum((residues * power[n + 1])[:, None, None] * pole_state, axis=0)
        for n in range(STEPS)
    ]
    weight = [jnp.sum(residues * power[j]) for j in range(STEPS)]

    history_cur = cur_hist
    history_ret = ret_hist
    outputs = []
    for step in range(STEPS):
        outgoing = jnp.dot(send_pick, history_ret.reshape(HIST * tiles, width))
        incoming = lax.all_to_all(
            outgoing.reshape(groups, cap, width), "grp", split_axis=0, concat_axis=0, tiled=True
        ).reshape(slots, width)
        near_rows = jnp.einsum(
            "kmth,hb->kmtb", near_pick, history_cur.reshape(HIST * tiles, width)
        )
        near_field = jnp.einsum(
            "kmtb,kab->ta", near_rows, near_mats, preferred_element_type=F32
        )
        far_terms = jnp.einsum(
            "sb,kab->ksa", incoming, far_mats, preferred_element_type=F32
        ).astype(BF16)
        group_part = jnp.dot(
            reader_hits, far_terms.reshape(classes * slots, width), preferred_element_type=F32
        ).astype(BF16)
        parts = lax.all_to_all(
            group_part.reshape(owners, tiles, width), "own", split_axis=0, concat_axis=0, tiled=True
        )
        far_field = jnp.sum(parts.astype(F32), axis=0)
        right_side = (excitation[step].astype(F32) - near_field - far_field).astype(BF16)
        current_now = jnp.einsum(
            "tab,tb->ta", self_inverse, right_side, preferred_element_type=F32
        ).astype(BF16)
        current_now = lax.optimization_barrier(current_now)
        outputs.append(current_now)
        if step + 1 < STEPS:
            retarded = current_now.astype(F32) + tail[step]
            for back in range(step + 1):
                retarded = retarded + weight[back] * outputs[step - back].astype(F32)
            history_cur = jnp.concatenate([current_now[None], history_cur[:-1]], axis=0)
            history_ret = jnp.concatenate(
                [retarded.astype(BF16)[None], history_ret[:-1]], axis=0
            )
    pole_final = power[STEPS][:, None, None] * pole_state
    for step in range(STEPS):
        pole_final = pole_final + power[STEPS - 1 - step][:, None, None] * outputs[step].astype(
            F32
        )
    return (jnp.stack(outputs), pole_final)


def solution(mesh):
    in_specs = (
        P(None, ("grp", "own"), None),
        P(None, ("grp", "own"), None),
        P(None, ("grp", "own"), None),
        P(None, ("grp", "own"), None),
        P(("grp", "own"), None, None),
        P(),
        P(),
        P(),
        P(),
        P(None, ("grp", "own"), None),
        P(None, ("grp", "own"), None),
        P(("grp", "own"), None),
        P(("grp", "own"), None),
        P("grp", None, "own", None, None),
    )
    out_specs = (P(None, ("grp", "own"), None), P(None, ("grp", "own"), None))
    return jax.shard_map(body, mesh=mesh, in_specs=in_specs, out_specs=out_specs, check_vma=False)
```

```python
import functools

import jax
import jax.numpy as jnp
from jax import lax
from jax.experimental import pallas as pl
from jax.experimental.pallas import tpu as pltpu
from jax.sharding import PartitionSpec as P

STEPS = 4
HIST = 4
F32 = jnp.float32
BF16 = jnp.bfloat16
I32 = jnp.int32
LANES = 128
CONTRACT_LAST = (((1,), (1,)), ((), ()))
VMEM = pl.BlockSpec(memory_space=pltpu.VMEM)
SMEM = pl.BlockSpec(memory_space=pltpu.SMEM)


def halves_stacked(rows):
    return jnp.concatenate([rows[:, :LANES], rows[:, LANES:]], axis=0)


def first_kernel(dest_ref, delay_ref, ret_ref, pick_ref, out_ref):
    hist, tiles, width = ret_ref.shape
    rows = pick_ref.shape[0]
    cols = pick_ref.shape[1]
    repeat = cols // tiles
    dest = jnp.concatenate([dest_ref[...]] * repeat, axis=0)
    delay = jnp.concatenate([delay_ref[...]] * repeat, axis=0)
    shape = (cols, rows)
    at = lax.broadcasted_iota(I32, shape, 1)
    group = at // 4
    col = lax.broadcasted_iota(I32, (cols, 1), 0)
    col_delay = (col // tiles) % hist + 1
    col_half = col // (tiles * hist)
    named = jnp.zeros(shape, F32)
    timed = jnp.zeros(shape, F32)
    for j in range(dest.shape[1]):
        hit = dest[:, j : j + 1] == group
        named = jnp.where(hit, 1.0, named)
        timed = jnp.where(hit & (delay[:, j : j + 1] == col_delay), 1.0, timed)
    to = lax.broadcasted_iota(I32, (cols, cols), 0)
    of = lax.broadcasted_iota(I32, (cols, cols), 1)
    earlier = jnp.where((to // tiles == of // tiles) & (of < to), 1.0, 0.0).astype(BF16)
    before = lax.dot(earlier, named.astype(BF16), preferred_element_type=F32)
    keep = (before == (at % 2).astype(F32)) & (col_half == (at // 2) % 2)
    pick = jnp.where(keep, timed, 0.0).T.astype(BF16)
    pick_ref[...] = pick
    stacked = halves_stacked(ret_ref[...].reshape(hist * tiles, width))
    out_ref[...] = lax.dot(pick, stacked, preferred_element_type=F32).astype(BF16)


def far_kernel(
    in_ref, split_ref, far_ref, hits_ref, near_pick_ref, cur_ref, near_ref, exc_ref,
    part_ref, base_ref, terms_ref,
):
    slots = split_ref.shape[1]
    incoming = in_ref[...]
    entries = jnp.concatenate(
        [
            lax.dot(split_ref[h], incoming, preferred_element_type=F32).astype(BF16)
            for h in range(2)
        ],
        axis=1,
    )
    for k in range(far_ref.shape[0]):
        terms = lax.dot_general(entries, far_ref[k], CONTRACT_LAST, preferred_element_type=F32)
        terms_ref[pl.ds(k * slots, slots), :] = terms.astype(BF16)
    near_rows = lax.dot(near_pick_ref[...], cur_ref[...], preferred_element_type=F32).astype(BF16)
    classes = near_ref.shape[0]
    tiles = exc_ref.shape[0]
    per_class = near_rows.shape[0] // classes
    base = exc_ref[...].astype(F32)
    for k in range(classes):
        near = lax.dot_general(
            near_rows[k * per_class : (k + 1) * per_class],
            near_ref[k],
            CONTRACT_LAST,
            preferred_element_type=F32,
        )
        for m in range(per_class // tiles):
            base = base - near[m * tiles : (m + 1) * tiles]
    base_ref[...] = base
    part_ref[...] = lax.dot(
        hits_ref[...], terms_ref[...], preferred_element_type=F32
    ).astype(BF16)


def solve(parts_ref, base_ref, inverse_ref):
    far_field = parts_ref[0].astype(F32)
    for o in range(1, parts_ref.shape[0]):
        far_field = far_field + parts_ref[o].astype(F32)
    right_side = (base_ref[...] - far_field).astype(BF16)
    tiles = right_side.shape[0]
    row = lax.broadcasted_iota(I32, right_side.shape, 0)
    current = jnp.zeros(right_side.shape, F32)
    for t in range(tiles):
        current = jnp.where(
            row == t, lax.dot(right_side, inverse_ref[t], preferred_element_type=F32), current
        )
    return current.astype(BF16)


def step_kernel(
    step, weight_ref, parts_ref, base_ref, inverse_ref, tail_ref, cur_ref, ret_ref, pick_ref,
    cur_out, ret_out, send_ref,
):
    current = solve(parts_ref, base_ref, inverse_ref)
    tiles = current.shape[0]
    wide = current.astype(F32)
    retarded = wide * (1.0 + weight_ref[0]) + tail_ref[step]
    for back in range(1, step + 1):
        past = cur_ref[pl.ds((back - 1) * tiles, tiles), :]
        retarded = retarded + weight_ref[back] * past.astype(F32)
    kept = cur_ref.shape[0] - tiles
    cur_out[...] = jnp.concatenate([current, cur_ref[:kept, :]], axis=0)
    history = jnp.concatenate([retarded.astype(BF16), ret_ref[:kept, :]], axis=0)
    ret_out[...] = history
    send_ref[...] = lax.dot(
        pick_ref[...], halves_stacked(history), preferred_element_type=F32
    ).astype(BF16)


def last_kernel(pole_ref, parts_ref, base_ref, inverse_ref, cur_ref, state_ref, cur_out, state_out):
    current = solve(parts_ref, base_ref, inverse_ref)
    tiles = current.shape[0]
    past = [cur_ref[pl.ds((STEPS - 2 - n) * tiles, tiles), :] for n in range(STEPS - 1)] + [current]
    for n in range(STEPS):
        cur_out[n] = past[n]
    wide = [c.astype(F32) for c in past]
    for p in range(state_ref.shape[0]):
        pole = pole_ref[p]
        state = state_ref[p]
        for n in range(STEPS):
            state = pole * state + wide[n]
        state_out[p] = state


def call(kernel, name, outs, specs, scratch=()):
    return pl.pallas_call(
        kernel,
        name=name,
        out_shape=outs,
        in_specs=specs,
        out_specs=jax.tree.map(lambda _: VMEM, outs),
        scratch_shapes=scratch,
        compiler_params=pltpu.CompilerParams(vmem_limit_bytes=8 << 20),
    )


def body(
    excitation,
    cur_hist,
    ret_hist,
    pole_state,
    self_inverse,
    near_mats,
    far_mats,
    poles,
    residues,
    near_src,
    near_delay,
    far_dest,
    far_delay,
    far_reader,
):
    groups = far_reader.shape[1]
    cap = far_reader.shape[3]
    classes = far_reader.shape[4]
    tiles = excitation.shape[1]
    width = excitation.shape[2]
    owners = lax.axis_size("own")
    group_tiles = tiles * owners
    slots = groups * cap
    past = HIST * tiles
    shape = jax.ShapeDtypeStruct

    pick, outgoing = call(
        first_kernel,
        "first",
        (shape((2 * slots, 2 * past), BF16), shape((2 * slots, LANES), BF16)),
        [VMEM] * 3,
    )(far_dest, far_delay, ret_hist)

    readers = far_reader.reshape(slots, classes)
    reader_hits = (
        readers.T[None, :, :] == jnp.arange(group_tiles, dtype=I32)[:, None, None]
    ).astype(BF16)
    reader_hits = reader_hits.reshape(group_tiles, classes * slots)
    slot = lax.broadcasted_iota(I32, (2, slots, 2 * slots), 1)
    half = lax.broadcasted_iota(I32, (2, slots, 2 * slots), 0)
    row = lax.broadcasted_iota(I32, (2, slots, 2 * slots), 2)
    split = (row == 4 * (slot // 2) + 2 * half + slot % 2).astype(BF16)
    near_row = ((near_delay - 1) * tiles + near_src).transpose(0, 2, 1).reshape(-1)
    near_pick = (near_row[:, None] == jnp.arange(past, dtype=I32)).astype(BF16)
    scale = [residues]
    for _ in range(STEPS - 1):
        scale.append(scale[-1] * poles)
    scale = jnp.stack(scale)
    weight = jnp.sum(scale, axis=1)
    tail = jnp.sum(scale[1:, :, None, None] * pole_state[None], axis=1)
    inverse = self_inverse.swapaxes(1, 2)

    current = cur_hist.reshape(past, width)
    retarded = ret_hist.reshape(past, width)
    for step in range(STEPS):
        incoming = lax.all_to_all(
            outgoing.reshape(groups, 2 * cap, LANES), "grp", split_axis=0, concat_axis=0, tiled=True
        ).reshape(2 * slots, LANES)
        if step == 0:
            incoming, inverse, tail, weight, reader_hits, near_pick, split = (
                lax.optimization_barrier(
                    (incoming, inverse, tail, weight, reader_hits, near_pick, split)
                )
            )
        part, base = call(
            far_kernel,
            "far",
            (shape((group_tiles, width), BF16), shape((tiles, width), F32)),
            [VMEM] * 8,
            [pltpu.VMEM((classes * slots, width), BF16)],
        )(
            incoming, split, far_mats, reader_hits, near_pick, current, near_mats, excitation[step]
        )
        parts = lax.all_to_all(
            part.reshape(owners, tiles, width), "own", split_axis=0, concat_axis=0, tiled=True
        )
        if step + 1 < STEPS:
            current, retarded, outgoing = call(
                functools.partial(step_kernel, step),
                "step",
                (
                    shape((past, width), BF16),
                    shape((past, width), BF16),
                    shape((2 * slots, LANES), BF16),
                ),
                [SMEM] + [VMEM] * 7,
            )(weight, parts, base, inverse, tail, current, retarded, pick)
    return call(
        last_kernel,
        "last",
        (shape((STEPS, tiles, width), BF16), shape(pole_state.shape, F32)),
        [SMEM] + [VMEM] * 5,
    )(poles, parts, base, inverse, current, pole_state)


def solution(mesh):
    in_specs = (
        P(None, ("grp", "own"), None),
        P(None, ("grp", "own"), None),
        P(None, ("grp", "own"), None),
        P(None, ("grp", "own"), None),
        P(("grp", "own"), None, None),
        P(),
        P(),
        P(),
        P(),
        P(None, ("grp", "own"), None),
        P(None, ("grp", "own"), None),
        P(("grp", "own"), None),
        P(("grp", "own"), None),
        P("grp", None, "own", None, None),
    )
    out_specs = (P(None, ("grp", "own"), None), P(None, ("grp", "own"), None))
    return jax.shard_map(body, mesh=mesh, in_specs=in_specs, out_specs=out_specs, check_vma=False)
```

```python
import functools

import jax
import jax.numpy as jnp
from jax import lax
from jax.experimental import pallas as pl
from jax.experimental.pallas import tpu as pltpu
from jax.sharding import PartitionSpec as P

STEPS = 4
HIST = 4
F32 = jnp.float32
BF16 = jnp.bfloat16
I32 = jnp.int32
LANES = 128
FAR_PIECES = 4
CONTRACT_LAST = (((1,), (1,)), ((), ()))
VMEM = pl.BlockSpec(memory_space=pltpu.VMEM)
HBM = pl.BlockSpec(memory_space=pltpu.HBM)
SMEM = pl.BlockSpec(memory_space=pltpu.SMEM)


def halves_stacked(rows):
    return jnp.concatenate([rows[:, :LANES], rows[:, LANES:]], axis=0)


def shifted(x, bits):
    return lax.shift_right_logical(x, jnp.full(x.shape, bits, x.dtype))


def first_kernel(
    dest_hbm, delay_hbm, ret_hbm, pick_ref, out_ref, dest_ref, delay_ref, ret_ref, sem
):
    copies = [
        pltpu.make_async_copy(src, dst, sem.at[n])
        for n, (src, dst) in enumerate(
            ((dest_hbm, dest_ref), (delay_hbm, delay_ref), (ret_hbm, ret_ref))
        )
    ]
    for copy in copies:
        copy.start()
    names, tiles = dest_ref.shape
    shape = pick_ref.shape
    rows, cols = shape
    at = lax.broadcasted_iota(I32, shape, 0)
    col = lax.broadcasted_iota(I32, (1, cols), 1)
    tile_bits = tiles.bit_length() - 1
    group = shifted(at, 2)
    slab = shifted(col, tile_bits)
    col_delay = (slab & (HIST - 1)) + 1
    col_half = shifted(col, tile_bits + HIST.bit_length() - 1)
    spread = jnp.where(
        lax.broadcasted_iota(I32, (tiles, cols), 0) == (col & (tiles - 1)), 1.0, 0.0
    ).astype(BF16)
    of = lax.broadcasted_iota(I32, (cols, cols), 0)
    earlier = jnp.where((shifted(of, tile_bits) == slab) & (of < col), 1.0, 0.0).astype(BF16)
    placed = (col_half == (shifted(at, 1) & 1)).astype(F32)
    rank = (at & 1).astype(F32)
    copies[0].wait()
    copies[1].wait()
    dest = lax.dot(dest_ref[...].astype(F32).astype(BF16), spread, preferred_element_type=F32)
    delay = lax.dot(delay_ref[...].astype(F32).astype(BF16), spread, preferred_element_type=F32)
    dest = dest.astype(I32)
    on_time = delay.astype(I32) == col_delay
    dest_on_time = jnp.where(on_time, dest, -1)
    named = jnp.zeros(shape, F32)
    timed = jnp.zeros(shape, F32)
    for j in range(names):
        named = jnp.where(dest[j : j + 1] == group, 1.0, named)
        timed = jnp.where(dest_on_time[j : j + 1] == group, placed, timed)
    before = lax.dot(named.astype(BF16), earlier, preferred_element_type=F32)
    pick = jnp.where(before == rank, timed, 0.0).astype(BF16)
    pick_ref[...] = pick
    copies[2].wait()
    out_ref[...] = lax.dot(
        pick, halves_stacked(ret_ref[...]), preferred_element_type=F32
    ).astype(BF16)


def tables_kernel(
    pole_ref, residue_ref, reader_ref, src_ref, delay_ref, state_ref,
    hits_ref, split_ref, near_pick_ref, tail_ref, coef_ref,
):
    cap, classes, groups = reader_ref.shape
    slots = cap * groups
    group_tiles = hits_ref.shape[0]
    readers = jnp.concatenate([reader_ref[c] for c in range(cap)], axis=1)
    place = lax.broadcasted_iota(I32, (group_tiles, slots), 0)
    for k in range(classes):
        hits_ref[:, k * slots : (k + 1) * slots] = jnp.where(
            place == readers[k : k + 1], 1.0, 0.0
        ).astype(BF16)
    slot = lax.broadcasted_iota(I32, (slots, 1), 0)
    row = lax.broadcasted_iota(I32, split_ref.shape[1:], 1)
    group_bits = groups.bit_length() - 1
    start = 4 * (slot & (groups - 1)) + shifted(slot, group_bits)
    for h in range(2):
        split_ref[h] = jnp.where(row == start + 2 * h, 1.0, 0.0).astype(BF16)
    sources, tiles = src_ref.shape
    near_row = ((delay_ref[...] - 1) * tiles + src_ref[...]).astype(F32).astype(BF16)
    eye = jnp.where(
        lax.broadcasted_iota(I32, (tiles, tiles), 0) == lax.broadcasted_iota(I32, (tiles, tiles), 1),
        1.0,
        0.0,
    ).astype(BF16)
    near_col = lax.dot_general(eye, near_row, CONTRACT_LAST, preferred_element_type=F32)
    near_col = near_col.astype(I32)
    at = lax.broadcasted_iota(I32, (tiles, near_pick_ref.shape[1]), 1)
    near_pick_ref[...] = jnp.concatenate(
        [jnp.where(at == near_col[:, a : a + 1], 1.0, 0.0) for a in range(sources)], axis=0
    ).astype(BF16)
    count = state_ref.shape[0]
    scale = [residue_ref[p] for p in range(count)]
    width = coef_ref.shape[1]
    for n in range(STEPS):
        total = scale[0]
        for p in range(1, count):
            total = total + scale[p]
        coef_ref[n : n + 1, :] = jnp.full((1, width), total, F32)
        if n + 1 < STEPS:
            scale = [scale[p] * pole_ref[p] for p in range(count)]
            tail = scale[0] * state_ref[0]
            for p in range(1, count):
                tail = tail + scale[p] * state_ref[p]
            tail_ref[n] = tail
    for p in range(count):
        coef_ref[8 + p : 9 + p, :] = jnp.full((1, width), pole_ref[p], F32)


def far_terms(entries, far_ref, terms_ref, first, last):
    slots = entries.shape[0]
    for k in range(first, last):
        terms = lax.dot_general(entries, far_ref[k], CONTRACT_LAST, preferred_element_type=F32)
        terms_ref[pl.ds(k * slots, slots), :] = terms.astype(BF16)


def entries_of(in_ref, split_ref):
    incoming = in_ref[...]
    return jnp.concatenate(
        [
            lax.dot(split_ref[h], incoming, preferred_element_type=F32).astype(BF16)
            for h in range(2)
        ],
        axis=1,
    )


def near_base(step, near_pick_ref, cur_ref, near_ref, exc_ref):
    near_rows = lax.dot(near_pick_ref[...], cur_ref[...], preferred_element_type=F32).astype(BF16)
    classes = near_ref.shape[0]
    tiles = exc_ref.shape[1]
    per_class = near_rows.shape[0] // classes
    base = exc_ref[step].astype(F32)
    for k in range(classes):
        near = lax.dot_general(
            near_rows[k * per_class : (k + 1) * per_class],
            near_ref[k],
            CONTRACT_LAST,
            preferred_element_type=F32,
        )
        for m in range(per_class // tiles):
            base = base - near[m * tiles : (m + 1) * tiles]
    return base


def far_first_kernel(
    in_ref, split_ref, far_hbm, hits_ref, near_pick_ref, cur_hbm, near_ref, exc_ref,
    part_ref, base_ref, far_ref, terms_ref, cur_ref, sem,
):
    size = far_ref.shape[0] // FAR_PIECES
    copies = [
        pltpu.make_async_copy(
            far_hbm.at[pl.ds(n * size, size)], far_ref.at[pl.ds(n * size, size)], sem.at[n]
        )
        for n in range(FAR_PIECES)
    ]
    current = pltpu.make_async_copy(cur_hbm, cur_ref, sem.at[FAR_PIECES])
    current.start()
    for copy in copies:
        copy.start()
    entries = entries_of(in_ref, split_ref)
    current.wait()
    base_ref[...] = near_base(0, near_pick_ref, cur_ref, near_ref, exc_ref)
    for n in range(FAR_PIECES):
        copies[n].wait()
        far_terms(entries, far_ref, terms_ref, n * size, (n + 1) * size)
    part_ref[...] = lax.dot(
        hits_ref[...], terms_ref[...], preferred_element_type=F32
    ).astype(BF16)


def far_kernel(
    step, in_ref, split_ref, far_ref, hits_ref, near_pick_ref, cur_ref, near_ref, exc_ref,
    part_ref, base_ref, terms_ref,
):
    far_terms(entries_of(in_ref, split_ref), far_ref, terms_ref, 0, far_ref.shape[0])
    base_ref[...] = near_base(step, near_pick_ref, cur_ref, near_ref, exc_ref)
    part_ref[...] = lax.dot(
        hits_ref[...], terms_ref[...], preferred_element_type=F32
    ).astype(BF16)


def solve(parts_ref, base_ref, inverse_ref):
    far_field = parts_ref[0].astype(F32)
    for o in range(1, parts_ref.shape[0]):
        far_field = far_field + parts_ref[o].astype(F32)
    right_side = (base_ref[...] - far_field).astype(BF16)
    tiles = right_side.shape[0]
    row = lax.broadcasted_iota(I32, right_side.shape, 0)
    current = jnp.zeros(right_side.shape, F32)
    for t in range(tiles):
        current = jnp.where(
            row == t, lax.dot(right_side, inverse_ref[t], preferred_element_type=F32), current
        )
    return current.astype(BF16)


def step_kernel(
    step, coef_ref, parts_ref, base_ref, inverse_ref, tail_ref, cur_ref, ret_ref, pick_ref,
    cur_out, send_ref, ret_out=None,
):
    current = solve(parts_ref, base_ref, inverse_ref)
    tiles = current.shape[0]
    wide = current.astype(F32)
    retarded = wide * (1.0 + coef_ref[0:1, :]) + tail_ref[step]
    for back in range(1, step + 1):
        past = cur_ref[pl.ds((back - 1) * tiles, tiles), :]
        retarded = retarded + coef_ref[back : back + 1, :] * past.astype(F32)
    kept = cur_ref.shape[0] - tiles
    cur_out[...] = jnp.concatenate([current, cur_ref[:kept, :]], axis=0)
    history = jnp.concatenate([retarded.astype(BF16), ret_ref[:kept, :]], axis=0)
    if ret_out is not None:
        ret_out[...] = history
    send_ref[...] = lax.dot(
        pick_ref[...], halves_stacked(history), preferred_element_type=F32
    ).astype(BF16)


def last_kernel(coef_ref, parts_ref, base_ref, inverse_ref, cur_ref, state_ref, cur_out, state_out):
    current = solve(parts_ref, base_ref, inverse_ref)
    tiles = current.shape[0]
    past = [cur_ref[pl.ds((STEPS - 2 - n) * tiles, tiles), :] for n in range(STEPS - 1)] + [current]
    for n in range(STEPS):
        cur_out[n] = past[n]
    wide = [c.astype(F32) for c in past]
    for p in range(state_ref.shape[0]):
        pole = coef_ref[8 + p : 9 + p, :]
        state = state_ref[p]
        for n in range(STEPS):
            state = pole * state + wide[n]
        state_out[p] = state


def in_hbm(x):
    return pltpu.with_memory_space_constraint(x, pltpu.HBM)


def call(kernel, name, outs, specs, scratch=()):
    return pl.pallas_call(
        kernel,
        name=name,
        out_shape=outs,
        in_specs=specs,
        out_specs=jax.tree.map(lambda _: VMEM, outs),
        scratch_shapes=scratch,
        compiler_params=pltpu.CompilerParams(vmem_limit_bytes=8 << 20),
    )


def body(
    excitation,
    cur_hist,
    ret_hist,
    pole_state,
    self_inverse,
    near_mats,
    far_mats,
    poles,
    residues,
    near_src,
    near_delay,
    far_dest,
    far_delay,
    far_reader,
):
    groups = far_reader.shape[1]
    cap = far_reader.shape[3]
    classes = far_reader.shape[4]
    tiles = excitation.shape[1]
    width = excitation.shape[2]
    owners = lax.axis_size("own")
    group_tiles = tiles * owners
    slots = groups * cap
    past = HIST * tiles
    shape = jax.ShapeDtypeStruct

    history = ret_hist.reshape(past, width)
    names = far_dest.shape[1]
    pick, outgoing = call(
        first_kernel,
        "first",
        (shape((2 * slots, 2 * past), BF16), shape((2 * slots, LANES), BF16)),
        [HBM] * 3,
        [
            pltpu.VMEM((names, tiles), I32),
            pltpu.VMEM((names, tiles), I32),
            pltpu.VMEM((past, width), BF16),
            pltpu.SemaphoreType.DMA((3,)),
        ],
    )(in_hbm(far_dest.T), in_hbm(far_delay.T), in_hbm(history))

    sources = near_src.shape[0] * near_src.shape[2]
    poles_count = poles.shape[0]
    reader_hits, split, near_pick, tail, coef = call(
        tables_kernel,
        "tables",
        (
            shape((group_tiles, classes * slots), BF16),
            shape((2, slots, 2 * slots), BF16),
            shape((sources * tiles, past), BF16),
            shape((STEPS - 1, tiles, width), F32),
            shape((8 + poles_count, width), F32),
        ),
        [SMEM] * 2 + [VMEM] * 4,
    )(
        in_hbm(poles),
        in_hbm(residues),
        far_reader[0, :, 0].transpose(1, 2, 0),
        near_src.transpose(0, 2, 1).reshape(sources, tiles),
        near_delay.transpose(0, 2, 1).reshape(sources, tiles),
        pole_state,
    )
    inverse = self_inverse.swapaxes(1, 2)

    current = cur_hist.reshape(past, width)
    retarded = history
    for step in range(STEPS):
        incoming = lax.all_to_all(
            outgoing.reshape(groups, 2 * cap, LANES), "grp", split_axis=0, concat_axis=0, tiled=True
        ).reshape(2 * slots, LANES)
        if step == 0:
            incoming, inverse, tail, coef, reader_hits, near_pick, split = (
                lax.optimization_barrier(
                    (incoming, inverse, tail, coef, reader_hits, near_pick, split)
                )
            )
        outs = (shape((group_tiles, width), BF16), shape((tiles, width), F32))
        terms = pltpu.VMEM((classes * slots, width), BF16)
        if step == 0:
            part, base, far_kept = call(
                far_first_kernel,
                "far",
                outs + (shape(far_mats.shape, BF16),),
                [VMEM] * 2 + [HBM] + [VMEM] * 2 + [HBM] + [VMEM] * 2,
                [
                    terms,
                    pltpu.VMEM((past, width), BF16),
                    pltpu.SemaphoreType.DMA((FAR_PIECES + 1,)),
                ],
            )(
                incoming, split, in_hbm(far_mats), reader_hits, near_pick, in_hbm(current),
                near_mats, excitation,
            )
        else:
            part, base = call(
                functools.partial(far_kernel, step), "far", outs, [VMEM] * 8, [terms]
            )(incoming, split, far_kept, reader_hits, near_pick, current, near_mats, excitation)
        parts = lax.all_to_all(
            part.reshape(owners, tiles, width), "own", split_axis=0, concat_axis=0, tiled=True
        )
        if step + 1 < STEPS:
            outs = (shape((past, width), BF16), shape((2 * slots, LANES), BF16))
            if step + 2 < STEPS:
                outs = outs + (shape((past, width), BF16),)
            made = call(
                functools.partial(step_kernel, step), "step", outs, [VMEM] * 8
            )(coef, parts, base, inverse, tail, current, retarded, pick)
            current, outgoing = made[:2]
            retarded = made[-1]
    return call(
        last_kernel,
        "last",
        (shape((STEPS, tiles, width), BF16), shape(pole_state.shape, F32)),
        [VMEM] * 6,
    )(coef, parts, base, inverse, current, pole_state)


def solution(mesh):
    in_specs = (
        P(None, ("grp", "own"), None),
        P(None, ("grp", "own"), None),
        P(None, ("grp", "own"), None),
        P(None, ("grp", "own"), None),
        P(("grp", "own"), None, None),
        P(),
        P(),
        P(),
        P(),
        P(None, ("grp", "own"), None),
        P(None, ("grp", "own"), None),
        P(("grp", "own"), None),
        P(("grp", "own"), None),
        P("grp", None, "own", None, None),
    )
    out_specs = (P(None, ("grp", "own"), None), P(None, ("grp", "own"), None))
    return jax.shard_map(body, mesh=mesh, in_specs=in_specs, out_specs=out_specs, check_vma=False)
```

```python
import functools

import jax
import jax.numpy as jnp
from jax import lax
from jax.experimental import pallas as pl
from jax.experimental.pallas import tpu as pltpu
from jax.sharding import PartitionSpec as P

STEPS = 4
HIST = 4
F32 = jnp.float32
BF16 = jnp.bfloat16
I32 = jnp.int32
LANES = 128
CONTRACT_LAST = (((1,), (1,)), ((), ()))
VMEM = pl.BlockSpec(memory_space=pltpu.VMEM)
HBM = pl.BlockSpec(memory_space=pltpu.HBM)


def halves_stacked(rows):
    return jnp.concatenate([rows[:, :LANES], rows[:, LANES:]], axis=0)


def shifted(x, bits):
    return lax.shift_right_logical(x, jnp.full(x.shape, bits, x.dtype))


def fetch(sem, *pairs):
    copies = [pltpu.make_async_copy(src, dst, sem.at[n]) for n, (src, dst) in enumerate(pairs)]
    for copy in copies:
        copy.start()
    return copies


def first_kernel(
    dest_hbm, delay_hbm, ret_hbm, pick_ref, out_ref, dest_ref, delay_ref, ret_ref, sem
):
    copies = fetch(sem, (dest_hbm, dest_ref), (delay_hbm, delay_ref), (ret_hbm, ret_ref))
    names, tiles = dest_ref.shape
    shape = pick_ref.shape
    rows, cols = shape
    at = lax.broadcasted_iota(I32, shape, 0)
    col = lax.broadcasted_iota(I32, (1, cols), 1)
    tile_bits = tiles.bit_length() - 1
    group = shifted(at, 2)
    slab = shifted(col, tile_bits)
    col_delay = (slab & (HIST - 1)) + 1
    col_half = shifted(col, tile_bits + HIST.bit_length() - 1)
    spread = jnp.where(
        lax.broadcasted_iota(I32, (tiles, cols), 0) == (col & (tiles - 1)), 1.0, 0.0
    ).astype(BF16)
    of = lax.broadcasted_iota(I32, (cols, cols), 0)
    earlier = jnp.where((shifted(of, tile_bits) == slab) & (of < col), 1.0, 0.0).astype(BF16)
    placed = (col_half == (shifted(at, 1) & 1)).astype(F32)
    rank = (at & 1).astype(F32)
    copies[0].wait()
    copies[1].wait()
    dest = lax.dot(dest_ref[...].astype(F32).astype(BF16), spread, preferred_element_type=F32)
    delay = lax.dot(delay_ref[...].astype(F32).astype(BF16), spread, preferred_element_type=F32)
    dest = dest.astype(I32)
    on_time = delay.astype(I32) == col_delay
    dest_on_time = jnp.where(on_time, dest, -1)
    named = jnp.zeros(shape, F32)
    timed = jnp.zeros(shape, F32)
    for j in range(names):
        named = jnp.where(dest[j : j + 1] == group, 1.0, named)
        timed = jnp.where(dest_on_time[j : j + 1] == group, placed, timed)
    before = lax.dot(named.astype(BF16), earlier, preferred_element_type=F32)
    pick = jnp.where(before == rank, timed, 0.0).astype(BF16)
    pick_ref[...] = pick
    copies[2].wait()
    out_ref[...] = lax.dot(
        pick, halves_stacked(ret_ref[...]), preferred_element_type=F32
    ).astype(BF16)


def tables_kernel(
    pole_hbm, residue_hbm, reader_hbm, src_hbm, delay_hbm, state_hbm, far_hbm,
    hits_ref, split_ref, near_pick_ref, tail_ref, coef_ref, far_ref,
    pole_ref, residue_ref, reader_ref, src_ref, delay_ref, state_ref, sem,
):
    reader_copy, src_copy, delay_copy, pole_copy, residue_copy, state_copy, far_copy = fetch(
        sem,
        (reader_hbm, reader_ref),
        (src_hbm, src_ref),
        (delay_hbm, delay_ref),
        (pole_hbm, pole_ref),
        (residue_hbm, residue_ref),
        (state_hbm, state_ref),
        (far_hbm, far_ref),
    )
    cap, classes, groups = reader_ref.shape
    slots = cap * groups
    group_tiles = hits_ref.shape[0]
    slot = lax.broadcasted_iota(I32, (slots, 1), 0)
    row = lax.broadcasted_iota(I32, split_ref.shape[1:], 1)
    group_bits = groups.bit_length() - 1
    start = 4 * (slot & (groups - 1)) + shifted(slot, group_bits)
    for h in range(2):
        split_ref[h] = jnp.where(row == start + 2 * h, 1.0, 0.0).astype(BF16)
    reader_copy.wait()
    readers = jnp.concatenate([reader_ref[c] for c in range(cap)], axis=1)
    place = lax.broadcasted_iota(I32, (group_tiles, slots), 0)
    for k in range(classes):
        hits_ref[:, k * slots : (k + 1) * slots] = jnp.where(
            place == readers[k : k + 1], 1.0, 0.0
        ).astype(BF16)
    src_copy.wait()
    delay_copy.wait()
    sources, tiles = src_ref.shape
    near_row = ((delay_ref[...] - 1) * tiles + src_ref[...]).astype(F32).astype(BF16)
    eye = jnp.where(
        lax.broadcasted_iota(I32, (tiles, tiles), 0) == lax.broadcasted_iota(I32, (tiles, tiles), 1),
        1.0,
        0.0,
    ).astype(BF16)
    near_col = lax.dot_general(eye, near_row, CONTRACT_LAST, preferred_element_type=F32)
    near_col = near_col.astype(I32)
    at = lax.broadcasted_iota(I32, (tiles, near_pick_ref.shape[1]), 1)
    near_pick_ref[...] = jnp.concatenate(
        [jnp.where(at == near_col[:, a : a + 1], 1.0, 0.0) for a in range(sources)], axis=0
    ).astype(BF16)
    pole_copy.wait()
    residue_copy.wait()
    state_copy.wait()
    count = state_ref.shape[0]
    scale = [residue_ref[p] for p in range(count)]
    width = coef_ref.shape[1]
    for n in range(STEPS):
        total = scale[0]
        for p in range(1, count):
            total = total + scale[p]
        coef_ref[n : n + 1, :] = jnp.full((1, width), total, F32)
        if n + 1 < STEPS:
            scale = [scale[p] * pole_ref[p] for p in range(count)]
            tail = scale[0] * state_ref[0]
            for p in range(1, count):
                tail = tail + scale[p] * state_ref[p]
            tail_ref[n] = tail
    for p in range(count):
        coef_ref[8 + p : 9 + p, :] = jnp.full((1, width), pole_ref[p], F32)
    far_copy.wait()


def far_terms(entries, far_ref, terms_ref, first, last):
    slots = entries.shape[0]
    for k in range(first, last):
        terms = lax.dot_general(entries, far_ref[k], CONTRACT_LAST, preferred_element_type=F32)
        terms_ref[pl.ds(k * slots, slots), :] = terms.astype(BF16)


def entries_of(in_ref, split_ref):
    incoming = in_ref[...]
    return jnp.concatenate(
        [
            lax.dot(split_ref[h], incoming, preferred_element_type=F32).astype(BF16)
            for h in range(2)
        ],
        axis=1,
    )


def near_base(step, near_pick_ref, cur_ref, near_ref, exc_ref):
    near_rows = lax.dot(near_pick_ref[...], cur_ref[...], preferred_element_type=F32).astype(BF16)
    classes = near_ref.shape[0]
    tiles = exc_ref.shape[1]
    per_class = near_rows.shape[0] // classes
    base = exc_ref[step].astype(F32)
    for k in range(classes):
        near = lax.dot_general(
            near_rows[k * per_class : (k + 1) * per_class],
            near_ref[k],
            CONTRACT_LAST,
            preferred_element_type=F32,
        )
        for m in range(per_class // tiles):
            base = base - near[m * tiles : (m + 1) * tiles]
    return base


def far_first_kernel(
    in_ref, split_ref, far_ref, hits_ref, near_pick_ref, cur_hbm, near_hbm, exc_hbm,
    inverse_hbm, part_ref, base_ref, inverse_ref, terms_ref, cur_ref, near_ref, exc_ref, sem,
):
    copies = fetch(sem, (cur_hbm, cur_ref), (near_hbm, near_ref), (exc_hbm, exc_ref))
    inverse_copy = pltpu.make_async_copy(inverse_hbm, inverse_ref, sem.at[len(copies)])
    inverse_copy.start()
    far_terms(entries_of(in_ref, split_ref), far_ref, terms_ref, 0, far_ref.shape[0])
    for copy in copies:
        copy.wait()
    base_ref[...] = near_base(0, near_pick_ref, cur_ref, near_ref, exc_ref)
    part_ref[...] = lax.dot(
        hits_ref[...], terms_ref[...], preferred_element_type=F32
    ).astype(BF16)
    inverse_copy.wait()


def far_kernel(
    step, in_ref, split_ref, far_ref, hits_ref, near_pick_ref, cur_ref, near_ref, exc_ref,
    part_ref, base_ref, terms_ref,
):
    far_terms(entries_of(in_ref, split_ref), far_ref, terms_ref, 0, far_ref.shape[0])
    base_ref[...] = near_base(step, near_pick_ref, cur_ref, near_ref, exc_ref)
    part_ref[...] = lax.dot(
        hits_ref[...], terms_ref[...], preferred_element_type=F32
    ).astype(BF16)


def solve(parts_ref, base_ref, inverse_ref):
    far_field = parts_ref[0].astype(F32)
    for o in range(1, parts_ref.shape[0]):
        far_field = far_field + parts_ref[o].astype(F32)
    right_side = (base_ref[...] - far_field).astype(BF16)
    tiles = right_side.shape[0]
    row = lax.broadcasted_iota(I32, right_side.shape, 0)
    current = jnp.zeros(right_side.shape, F32)
    for t in range(tiles):
        current = jnp.where(
            row == t,
            lax.dot_general(
                right_side, inverse_ref[t], CONTRACT_LAST, preferred_element_type=F32
            ),
            current,
        )
    return current.astype(BF16)


def step_kernel(
    step, coef_ref, parts_ref, base_ref, inverse_ref, tail_ref, cur_ref, ret_ref, pick_ref,
    cur_out, send_ref, ret_out=None,
):
    current = solve(parts_ref, base_ref, inverse_ref)
    tiles = current.shape[0]
    wide = current.astype(F32)
    retarded = wide * (1.0 + coef_ref[0:1, :]) + tail_ref[step]
    for back in range(1, step + 1):
        past = cur_ref[pl.ds((back - 1) * tiles, tiles), :]
        retarded = retarded + coef_ref[back : back + 1, :] * past.astype(F32)
    kept = cur_ref.shape[0] - tiles
    cur_out[...] = jnp.concatenate([current, cur_ref[:kept, :]], axis=0)
    history = jnp.concatenate([retarded.astype(BF16), ret_ref[:kept, :]], axis=0)
    if ret_out is not None:
        ret_out[...] = history
    send_ref[...] = lax.dot(
        pick_ref[...], halves_stacked(history), preferred_element_type=F32
    ).astype(BF16)


def last_kernel(coef_ref, parts_ref, base_ref, inverse_ref, cur_ref, state_ref, cur_out, state_out):
    current = solve(parts_ref, base_ref, inverse_ref)
    tiles = current.shape[0]
    past = [cur_ref[pl.ds((STEPS - 2 - n) * tiles, tiles), :] for n in range(STEPS - 1)] + [current]
    for n in range(STEPS):
        cur_out[n] = past[n]
    wide = [c.astype(F32) for c in past]
    for p in range(state_ref.shape[0]):
        pole = coef_ref[8 + p : 9 + p, :]
        state = state_ref[p]
        for n in range(STEPS):
            state = pole * state + wide[n]
        state_out[p] = state


def in_hbm(x):
    return pltpu.with_memory_space_constraint(x, pltpu.HBM)


def call(kernel, name, outs, specs, scratch=()):
    return pl.pallas_call(
        kernel,
        name=name,
        out_shape=outs,
        in_specs=specs,
        out_specs=jax.tree.map(lambda _: VMEM, outs),
        scratch_shapes=scratch,
        compiler_params=pltpu.CompilerParams(vmem_limit_bytes=8 << 20),
    )


def body(
    excitation,
    cur_hist,
    ret_hist,
    pole_state,
    self_inverse,
    near_mats,
    far_mats,
    poles,
    residues,
    near_src,
    near_delay,
    far_dest,
    far_delay,
    far_reader,
):
    groups = far_reader.shape[1]
    cap = far_reader.shape[3]
    classes = far_reader.shape[4]
    tiles = excitation.shape[1]
    width = excitation.shape[2]
    owners = lax.axis_size("own")
    group_tiles = tiles * owners
    slots = groups * cap
    past = HIST * tiles
    shape = jax.ShapeDtypeStruct

    history = ret_hist.reshape(past, width)
    names = far_dest.shape[1]
    pick, outgoing = call(
        first_kernel,
        "first",
        (shape((2 * slots, 2 * past), BF16), shape((2 * slots, LANES), BF16)),
        [HBM] * 3,
        [
            pltpu.VMEM((names, tiles), I32),
            pltpu.VMEM((names, tiles), I32),
            pltpu.VMEM((past, width), BF16),
            pltpu.SemaphoreType.DMA((3,)),
        ],
    )(in_hbm(far_dest.T), in_hbm(far_delay.T), in_hbm(history))

    sources = near_src.shape[0] * near_src.shape[2]
    poles_count = poles.shape[0]
    reader_hits, split, near_pick, tail, coef, far_kept = call(
        tables_kernel,
        "tables",
        (
            shape((group_tiles, classes * slots), BF16),
            shape((2, slots, 2 * slots), BF16),
            shape((sources * tiles, past), BF16),
            shape((STEPS - 1, tiles, width), F32),
            shape((8 + poles_count, width), F32),
            shape(far_mats.shape, BF16),
        ),
        [HBM] * 7,
        [
            pltpu.SMEM((poles_count,), F32),
            pltpu.SMEM((poles_count,), F32),
            pltpu.VMEM((cap, classes, groups), I32),
            pltpu.VMEM((sources, tiles), I32),
            pltpu.VMEM((sources, tiles), I32),
            pltpu.VMEM(pole_state.shape, F32),
            pltpu.SemaphoreType.DMA((7,)),
        ],
    )(
        in_hbm(poles),
        in_hbm(residues),
        in_hbm(far_reader[0, :, 0].transpose(1, 2, 0)),
        in_hbm(near_src.transpose(0, 2, 1).reshape(sources, tiles)),
        in_hbm(near_delay.transpose(0, 2, 1).reshape(sources, tiles)),
        in_hbm(pole_state),
        in_hbm(far_mats),
    )

    current = cur_hist.reshape(past, width)
    retarded = history
    for step in range(STEPS):
        incoming = lax.all_to_all(
            outgoing.reshape(groups, 2 * cap, LANES), "grp", split_axis=0, concat_axis=0, tiled=True
        ).reshape(2 * slots, LANES)
        if step == 0:
            incoming, tail, coef, reader_hits, near_pick, split, far_kept = (
                lax.optimization_barrier(
                    (incoming, tail, coef, reader_hits, near_pick, split, far_kept)
                )
            )
        outs = (shape((group_tiles, width), BF16), shape((tiles, width), F32))
        terms = pltpu.VMEM((classes * slots, width), BF16)
        if step == 0:
            part, base, inverse = call(
                far_first_kernel,
                "far",
                outs + (shape(self_inverse.shape, BF16),),
                [VMEM] * 5 + [HBM] * 4,
                [
                    terms,
                    pltpu.VMEM((past, width), BF16),
                    pltpu.VMEM(near_mats.shape, BF16),
                    pltpu.VMEM(excitation.shape, BF16),
                    pltpu.SemaphoreType.DMA((4,)),
                ],
            )(
                incoming, split, far_kept, reader_hits, near_pick, in_hbm(current),
                in_hbm(near_mats), in_hbm(excitation), in_hbm(self_inverse),
            )
        else:
            part, base = call(
                functools.partial(far_kernel, step), "far", outs, [VMEM] * 8, [terms]
            )(incoming, split, far_kept, reader_hits, near_pick, current, near_mats, excitation)
        parts = lax.all_to_all(
            part.reshape(owners, tiles, width), "own", split_axis=0, concat_axis=0, tiled=True
        )
        if step + 1 < STEPS:
            outs = (shape((past, width), BF16), shape((2 * slots, LANES), BF16))
            if step + 2 < STEPS:
                outs = outs + (shape((past, width), BF16),)
            made = call(
                functools.partial(step_kernel, step), "step", outs, [VMEM] * 8
            )(coef, parts, base, inverse, tail, current, retarded, pick)
            current, outgoing = made[:2]
            retarded = made[-1]
    return call(
        last_kernel,
        "last",
        (shape((STEPS, tiles, width), BF16), shape(pole_state.shape, F32)),
        [VMEM] * 6,
    )(coef, parts, base, inverse, current, pole_state)


def solution(mesh):
    in_specs = (
        P(None, ("grp", "own"), None),
        P(None, ("grp", "own"), None),
        P(None, ("grp", "own"), None),
        P(None, ("grp", "own"), None),
        P(("grp", "own"), None, None),
        P(),
        P(),
        P(),
        P(),
        P(None, ("grp", "own"), None),
        P(None, ("grp", "own"), None),
        P(("grp", "own"), None),
        P(("grp", "own"), None),
        P("grp", None, "own", None, None),
    )
    out_specs = (P(None, ("grp", "own"), None), P(None, ("grp", "own"), None))
    return jax.shard_map(body, mesh=mesh, in_specs=in_specs, out_specs=out_specs, check_vma=False)
```

```python
import functools

import jax
import jax.numpy as jnp
from jax import lax
from jax.experimental import pallas as pl
from jax.experimental.pallas import tpu as pltpu
from jax.sharding import PartitionSpec as P

STEPS = 4
HIST = 4
F32 = jnp.float32
BF16 = jnp.bfloat16
I32 = jnp.int32
LANES = 128
FAR_PIECES = 4
CONTRACT_LAST = (((1,), (1,)), ((), ()))
VMEM = pl.BlockSpec(memory_space=pltpu.VMEM)
HBM = pl.BlockSpec(memory_space=pltpu.HBM)


def halves_stacked(rows):
    return jnp.concatenate([rows[:, :LANES], rows[:, LANES:]], axis=0)


def shifted(x, bits):
    return lax.shift_right_logical(x, jnp.full(x.shape, bits, x.dtype))


def fetch(sem, *pairs):
    copies = [pltpu.make_async_copy(src, dst, sem.at[n]) for n, (src, dst) in enumerate(pairs)]
    for copy in copies:
        copy.start()
    return copies


def first_kernel(
    dest_hbm, delay_hbm, ret_hbm, pick_ref, out_ref, dest_ref, delay_ref, ret_ref, sem
):
    copies = fetch(sem, (dest_hbm, dest_ref), (delay_hbm, delay_ref), (ret_hbm, ret_ref))
    names, tiles = dest_ref.shape
    shape = pick_ref.shape
    rows, cols = shape
    at = lax.broadcasted_iota(I32, shape, 0)
    col = lax.broadcasted_iota(I32, (1, cols), 1)
    tile_bits = tiles.bit_length() - 1
    group = shifted(at, 2)
    slab = shifted(col, tile_bits)
    col_delay = (slab & (HIST - 1)) + 1
    col_half = shifted(col, tile_bits + HIST.bit_length() - 1)
    spread = jnp.where(
        lax.broadcasted_iota(I32, (tiles, cols), 0) == (col & (tiles - 1)), 1.0, 0.0
    ).astype(BF16)
    of = lax.broadcasted_iota(I32, (cols, cols), 0)
    earlier = jnp.where((shifted(of, tile_bits) == slab) & (of < col), 1.0, 0.0).astype(BF16)
    placed = (col_half == (shifted(at, 1) & 1)).astype(F32)
    rank = (at & 1).astype(F32)
    copies[0].wait()
    copies[1].wait()
    dest = lax.dot(dest_ref[...].astype(F32).astype(BF16), spread, preferred_element_type=F32)
    delay = lax.dot(delay_ref[...].astype(F32).astype(BF16), spread, preferred_element_type=F32)
    dest = dest.astype(I32)
    on_time = delay.astype(I32) == col_delay
    dest_on_time = jnp.where(on_time, dest, -1)
    named = jnp.zeros(shape, F32)
    timed = jnp.zeros(shape, F32)
    for j in range(names):
        named = jnp.where(dest[j : j + 1] == group, 1.0, named)
        timed = jnp.where(dest_on_time[j : j + 1] == group, placed, timed)
    before = lax.dot(named.astype(BF16), earlier, preferred_element_type=F32)
    pick = jnp.where(before == rank, timed, 0.0).astype(BF16)
    pick_ref[...] = pick
    copies[2].wait()
    out_ref[...] = lax.dot(
        pick, halves_stacked(ret_ref[...]), preferred_element_type=F32
    ).astype(BF16)


def tables_kernel(
    pole_hbm, residue_hbm, reader_hbm, src_hbm, delay_hbm, state_hbm, far_hbm,
    hits_ref, split_ref, near_pick_ref, tail_ref, coef_ref, *rest,
):
    turned = rest[:FAR_PIECES]
    pole_ref, residue_ref, reader_ref, src_ref, delay_ref, state_ref, far_ref, sem = rest[FAR_PIECES:]
    size = far_ref.shape[0] // FAR_PIECES
    copies = fetch(
        sem,
        (reader_hbm, reader_ref),
        (src_hbm, src_ref),
        (delay_hbm, delay_ref),
        (pole_hbm, pole_ref),
        (residue_hbm, residue_ref),
        (state_hbm, state_ref),
        *(
            (far_hbm.at[pl.ds(n * size, size)], far_ref.at[pl.ds(n * size, size)])
            for n in range(FAR_PIECES)
        ),
    )
    reader_copy, src_copy, delay_copy, pole_copy, residue_copy, state_copy = copies[:6]
    cap, classes, groups = reader_ref.shape
    slots = cap * groups
    group_tiles = hits_ref.shape[0]
    slot = lax.broadcasted_iota(I32, (slots, 1), 0)
    row = lax.broadcasted_iota(I32, split_ref.shape[1:], 1)
    group_bits = groups.bit_length() - 1
    start = 4 * (slot & (groups - 1)) + shifted(slot, group_bits)
    for h in range(2):
        split_ref[h] = jnp.where(row == start + 2 * h, 1.0, 0.0).astype(BF16)
    reader_copy.wait()
    readers = jnp.concatenate([reader_ref[c] for c in range(cap)], axis=1)
    place = lax.broadcasted_iota(I32, (group_tiles, slots), 0)
    for k in range(classes):
        hits_ref[:, k * slots : (k + 1) * slots] = jnp.where(
            place == readers[k : k + 1], 1.0, 0.0
        ).astype(BF16)
    src_copy.wait()
    delay_copy.wait()
    sources, tiles = src_ref.shape
    near_row = ((delay_ref[...] - 1) * tiles + src_ref[...]).astype(F32).astype(BF16)
    eye = jnp.where(
        lax.broadcasted_iota(I32, (tiles, tiles), 0) == lax.broadcasted_iota(I32, (tiles, tiles), 1),
        1.0,
        0.0,
    ).astype(BF16)
    near_col = lax.dot_general(eye, near_row, CONTRACT_LAST, preferred_element_type=F32)
    near_col = near_col.astype(I32)
    at = lax.broadcasted_iota(I32, (tiles, near_pick_ref.shape[1]), 1)
    near_pick_ref[...] = jnp.concatenate(
        [jnp.where(at == near_col[:, a : a + 1], 1.0, 0.0) for a in range(sources)], axis=0
    ).astype(BF16)
    pole_copy.wait()
    residue_copy.wait()
    state_copy.wait()
    count = state_ref.shape[0]
    scale = [residue_ref[p] for p in range(count)]
    width = coef_ref.shape[1]
    for n in range(STEPS):
        total = scale[0]
        for p in range(1, count):
            total = total + scale[p]
        coef_ref[n : n + 1, :] = jnp.full((1, width), total, F32)
        if n + 1 < STEPS:
            scale = [scale[p] * pole_ref[p] for p in range(count)]
            tail = scale[0] * state_ref[0]
            for p in range(1, count):
                tail = tail + scale[p] * state_ref[p]
            tail_ref[n] = tail
    for p in range(count):
        coef_ref[8 + p : 9 + p, :] = jnp.full((1, width), pole_ref[p], F32)
    for n in range(FAR_PIECES):
        copies[6 + n].wait()
        for k in range(size):
            turned[n][k] = far_ref[n * size + k].T


def far_terms(entries, turned, terms_ref):
    slots = entries.shape[0]
    at = 0
    for piece in turned:
        for k in range(piece.shape[0]):
            terms = lax.dot(entries, piece[k], preferred_element_type=F32)
            terms_ref[pl.ds(at, slots), :] = terms.astype(BF16)
            at += slots


def entries_of(in_ref, split_ref):
    incoming = in_ref[...]
    return jnp.concatenate(
        [
            lax.dot(split_ref[h], incoming, preferred_element_type=F32).astype(BF16)
            for h in range(2)
        ],
        axis=1,
    )


def near_base(step, near_pick_ref, cur_ref, near_ref, exc_ref):
    near_rows = lax.dot(near_pick_ref[...], cur_ref[...], preferred_element_type=F32).astype(BF16)
    classes = near_ref.shape[0]
    tiles = exc_ref.shape[1]
    per_class = near_rows.shape[0] // classes
    base = exc_ref[step].astype(F32)
    for k in range(classes):
        near = lax.dot_general(
            near_rows[k * per_class : (k + 1) * per_class],
            near_ref[k],
            CONTRACT_LAST,
            preferred_element_type=F32,
        )
        for m in range(per_class // tiles):
            base = base - near[m * tiles : (m + 1) * tiles]
    return base


def far_first_kernel(in_ref, split_ref, hits_ref, near_pick_ref, *rest):
    turned = rest[:FAR_PIECES]
    cur_hbm, near_hbm, exc_hbm, part_ref, base_ref = rest[FAR_PIECES : FAR_PIECES + 5]
    terms_ref, cur_ref, near_ref, exc_ref, sem = rest[FAR_PIECES + 5 :]
    copies = fetch(sem, (cur_hbm, cur_ref), (near_hbm, near_ref), (exc_hbm, exc_ref))
    far_terms(entries_of(in_ref, split_ref), turned, terms_ref)
    for copy in copies:
        copy.wait()
    base_ref[...] = near_base(0, near_pick_ref, cur_ref, near_ref, exc_ref)
    part_ref[...] = lax.dot(
        hits_ref[...], terms_ref[...], preferred_element_type=F32
    ).astype(BF16)


def far_kernel(step, in_ref, split_ref, hits_ref, near_pick_ref, *rest):
    turned = rest[:FAR_PIECES]
    cur_ref, near_ref, exc_ref, part_ref, base_ref, terms_ref = rest[FAR_PIECES:]
    far_terms(entries_of(in_ref, split_ref), turned, terms_ref)
    base_ref[...] = near_base(step, near_pick_ref, cur_ref, near_ref, exc_ref)
    part_ref[...] = lax.dot(
        hits_ref[...], terms_ref[...], preferred_element_type=F32
    ).astype(BF16)


def solve(parts_ref, base_ref, inverse_ref, turned_ref=None):
    far_field = parts_ref[0].astype(F32)
    for o in range(1, parts_ref.shape[0]):
        far_field = far_field + parts_ref[o].astype(F32)
    right_side = (base_ref[...] - far_field).astype(BF16)
    tiles = right_side.shape[0]
    row = lax.broadcasted_iota(I32, right_side.shape, 0)
    current = jnp.zeros(right_side.shape, F32)
    for t in range(tiles):
        turned = inverse_ref[t]
        if turned_ref is not None:
            turned = turned.T
            turned_ref[t] = turned
        current = jnp.where(
            row == t, lax.dot(right_side, turned, preferred_element_type=F32), current
        )
    return current.astype(BF16)


def step_kernel(
    step, coef_ref, parts_ref, base_ref, inverse_ref, tail_ref, cur_ref, ret_ref, pick_ref,
    cur_out, send_ref, ret_out=None, turned_ref=None,
):
    current = solve(parts_ref, base_ref, inverse_ref, turned_ref)
    tiles = current.shape[0]
    wide = current.astype(F32)
    retarded = wide * (1.0 + coef_ref[0:1, :]) + tail_ref[step]
    for back in range(1, step + 1):
        past = cur_ref[pl.ds((back - 1) * tiles, tiles), :]
        retarded = retarded + coef_ref[back : back + 1, :] * past.astype(F32)
    kept = cur_ref.shape[0] - tiles
    cur_out[...] = jnp.concatenate([current, cur_ref[:kept, :]], axis=0)
    history = jnp.concatenate([retarded.astype(BF16), ret_ref[:kept, :]], axis=0)
    if ret_out is not None:
        ret_out[...] = history
    send_ref[...] = lax.dot(
        pick_ref[...], halves_stacked(history), preferred_element_type=F32
    ).astype(BF16)


def last_kernel(coef_ref, parts_ref, base_ref, inverse_ref, cur_ref, state_ref, cur_out, state_out):
    current = solve(parts_ref, base_ref, inverse_ref)
    tiles = current.shape[0]
    past = [cur_ref[pl.ds((STEPS - 2 - n) * tiles, tiles), :] for n in range(STEPS - 1)] + [current]
    for n in range(STEPS):
        cur_out[n] = past[n]
    wide = [c.astype(F32) for c in past]
    for p in range(state_ref.shape[0]):
        pole = coef_ref[8 + p : 9 + p, :]
        state = state_ref[p]
        for n in range(STEPS):
            state = pole * state + wide[n]
        state_out[p] = state


def in_hbm(x):
    return pltpu.with_memory_space_constraint(x, pltpu.HBM)


def call(kernel, name, outs, specs, scratch=()):
    return pl.pallas_call(
        kernel,
        name=name,
        out_shape=outs,
        in_specs=specs,
        out_specs=jax.tree.map(lambda _: VMEM, outs),
        scratch_shapes=scratch,
        compiler_params=pltpu.CompilerParams(vmem_limit_bytes=8 << 20),
    )


def body(
    excitation,
    cur_hist,
    ret_hist,
    pole_state,
    self_inverse,
    near_mats,
    far_mats,
    poles,
    residues,
    near_src,
    near_delay,
    far_dest,
    far_delay,
    far_reader,
):
    groups = far_reader.shape[1]
    cap = far_reader.shape[3]
    classes = far_reader.shape[4]
    tiles = excitation.shape[1]
    width = excitation.shape[2]
    owners = lax.axis_size("own")
    group_tiles = tiles * owners
    slots = groups * cap
    past = HIST * tiles
    shape = jax.ShapeDtypeStruct

    history = ret_hist.reshape(past, width)
    names = far_dest.shape[1]
    pick, outgoing = call(
        first_kernel,
        "first",
        (shape((2 * slots, 2 * past), BF16), shape((2 * slots, LANES), BF16)),
        [HBM] * 3,
        [
            pltpu.VMEM((names, tiles), I32),
            pltpu.VMEM((names, tiles), I32),
            pltpu.VMEM((past, width), BF16),
            pltpu.SemaphoreType.DMA((3,)),
        ],
    )(in_hbm(far_dest.T), in_hbm(far_delay.T), in_hbm(history))

    sources = near_src.shape[0] * near_src.shape[2]
    poles_count = poles.shape[0]
    reader_hits, split, near_pick, tail, coef, *turned = call(
        tables_kernel,
        "tables",
        (
            shape((group_tiles, classes * slots), BF16),
            shape((2, slots, 2 * slots), BF16),
            shape((sources * tiles, past), BF16),
            shape((STEPS - 1, tiles, width), F32),
            shape((8 + poles_count, width), F32),
            *[shape((classes // FAR_PIECES, width, width), BF16)] * FAR_PIECES,
        ),
        [HBM] * 7,
        [
            pltpu.SMEM((poles_count,), F32),
            pltpu.SMEM((poles_count,), F32),
            pltpu.VMEM((cap, classes, groups), I32),
            pltpu.VMEM((sources, tiles), I32),
            pltpu.VMEM((sources, tiles), I32),
            pltpu.VMEM(pole_state.shape, F32),
            pltpu.VMEM(far_mats.shape, BF16),
            pltpu.SemaphoreType.DMA((6 + FAR_PIECES,)),
        ],
    )(
        in_hbm(poles),
        in_hbm(residues),
        in_hbm(far_reader[0, :, 0].transpose(1, 2, 0)),
        in_hbm(near_src.transpose(0, 2, 1).reshape(sources, tiles)),
        in_hbm(near_delay.transpose(0, 2, 1).reshape(sources, tiles)),
        in_hbm(pole_state),
        in_hbm(far_mats),
    )

    current = cur_hist.reshape(past, width)
    inverse = self_inverse
    retarded = history
    for step in range(STEPS):
        incoming = lax.all_to_all(
            outgoing.reshape(groups, 2 * cap, LANES), "grp", split_axis=0, concat_axis=0, tiled=True
        ).reshape(2 * slots, LANES)
        if step == 0:
            incoming, tail, coef, reader_hits, near_pick, split, *turned = (
                lax.optimization_barrier(
                    (incoming, tail, coef, reader_hits, near_pick, split, *turned)
                )
            )
        outs = (shape((group_tiles, width), BF16), shape((tiles, width), F32))
        terms = pltpu.VMEM((classes * slots, width), BF16)
        kept = (incoming, split, reader_hits, near_pick, *turned)
        if step == 0:
            part, base = call(
                far_first_kernel,
                "far",
                outs,
                [VMEM] * len(kept) + [HBM] * 3,
                [
                    terms,
                    pltpu.VMEM((past, width), BF16),
                    pltpu.VMEM(near_mats.shape, BF16),
                    pltpu.VMEM(excitation.shape, BF16),
                    pltpu.SemaphoreType.DMA((3,)),
                ],
            )(*kept, in_hbm(current), in_hbm(near_mats), in_hbm(excitation))
        else:
            part, base = call(
                functools.partial(far_kernel, step),
                "far",
                outs,
                [VMEM] * (len(kept) + 3),
                [terms],
            )(*kept, current, near_mats, excitation)
        parts = lax.all_to_all(
            part.reshape(owners, tiles, width), "own", split_axis=0, concat_axis=0, tiled=True
        )
        if step + 1 < STEPS:
            outs = (shape((past, width), BF16), shape((2 * slots, LANES), BF16))
            if step + 2 < STEPS:
                outs = outs + (shape((past, width), BF16),)
            if step == 0:
                outs = outs + (shape(self_inverse.shape, BF16),)
            made = call(functools.partial(step_kernel, step), "step", outs, [VMEM] * 8)(
                coef, parts, base, inverse, tail, current, retarded, pick
            )
            current, outgoing = made[:2]
            if step + 2 < STEPS:
                retarded = made[2]
            if step == 0:
                inverse = made[3]
    return call(
        last_kernel,
        "last",
        (shape((STEPS, tiles, width), BF16), shape(pole_state.shape, F32)),
        [VMEM] * 6,
    )(coef, parts, base, inverse, current, pole_state)


def solution(mesh):
    in_specs = (
        P(None, ("grp", "own"), None),
        P(None, ("grp", "own"), None),
        P(None, ("grp", "own"), None),
        P(None, ("grp", "own"), None),
        P(("grp", "own"), None, None),
        P(),
        P(),
        P(),
        P(),
        P(None, ("grp", "own"), None),
        P(None, ("grp", "own"), None),
        P(("grp", "own"), None),
        P(("grp", "own"), None),
        P("grp", None, "own", None, None),
    )
    out_specs = (P(None, ("grp", "own"), None), P(None, ("grp", "own"), None))
    return jax.shard_map(body, mesh=mesh, in_specs=in_specs, out_specs=out_specs, check_vma=False)
```

```python
import functools

import jax
import jax.numpy as jnp
from jax import lax
from jax.experimental import pallas as pl
from jax.experimental.pallas import tpu as pltpu
from jax.sharding import PartitionSpec as P

STEPS = 4
HIST = 4
F32 = jnp.float32
BF16 = jnp.bfloat16
I32 = jnp.int32
LANES = 128
FAR_PIECES = 4
CONTRACT_LAST = (((1,), (1,)), ((), ()))
VMEM = pl.BlockSpec(memory_space=pltpu.VMEM)
HBM = pl.BlockSpec(memory_space=pltpu.HBM)


def halves_stacked(rows):
    return jnp.concatenate([rows[:, :LANES], rows[:, LANES:]], axis=0)


def shifted(x, bits):
    return lax.shift_right_logical(x, jnp.full(x.shape, bits, x.dtype))


def fetch(sem, *pairs):
    copies = [pltpu.make_async_copy(src, dst, sem.at[n]) for n, (src, dst) in enumerate(pairs)]
    for copy in copies:
        copy.start()
    return copies


def first_kernel(
    dest_hbm, delay_hbm, ret_hbm, pick_ref, out_ref, dest_ref, delay_ref, ret_ref, sem
):
    copies = fetch(sem, (dest_hbm, dest_ref), (delay_hbm, delay_ref), (ret_hbm, ret_ref))
    names, tiles = dest_ref.shape
    shape = pick_ref.shape
    rows, cols = shape
    at = lax.broadcasted_iota(I32, shape, 0)
    col = lax.broadcasted_iota(I32, (1, cols), 1)
    tile_bits = tiles.bit_length() - 1
    group = shifted(at, 2)
    slab = shifted(col, tile_bits)
    col_delay = (slab & (HIST - 1)) + 1
    col_half = shifted(col, tile_bits + HIST.bit_length() - 1)
    spread = jnp.where(
        lax.broadcasted_iota(I32, (tiles, cols), 0) == (col & (tiles - 1)), 1.0, 0.0
    ).astype(BF16)
    of = lax.broadcasted_iota(I32, (cols, cols), 0)
    earlier = jnp.where((shifted(of, tile_bits) == slab) & (of < col), 1.0, 0.0).astype(BF16)
    placed = (col_half == (shifted(at, 1) & 1)).astype(F32)
    rank = (at & 1).astype(F32)
    copies[0].wait()
    copies[1].wait()
    dest = lax.dot(dest_ref[...].astype(F32).astype(BF16), spread, preferred_element_type=F32)
    delay = lax.dot(delay_ref[...].astype(F32).astype(BF16), spread, preferred_element_type=F32)
    dest = dest.astype(I32)
    on_time = delay.astype(I32) == col_delay
    dest_on_time = jnp.where(on_time, dest, -1)
    named = jnp.zeros(shape, F32)
    timed = jnp.zeros(shape, F32)
    for j in range(names):
        named = jnp.where(dest[j : j + 1] == group, 1.0, named)
        timed = jnp.where(dest_on_time[j : j + 1] == group, placed, timed)
    before = lax.dot(named.astype(BF16), earlier, preferred_element_type=F32)
    pick = jnp.where(before == rank, timed, 0.0).astype(BF16)
    pick_ref[...] = pick
    copies[2].wait()
    out_ref[...] = lax.dot(
        pick, halves_stacked(ret_ref[...]), preferred_element_type=F32
    ).astype(BF16)


def tables_kernel(
    pole_hbm, residue_hbm, reader_hbm, src_hbm, delay_hbm, state_hbm, far_hbm,
    cur_hbm, near_hbm, exc_hbm, hits_ref, split_ref, near_pick_ref, tail_ref, coef_ref, base_ref,
    *rest,
):
    turned = rest[:FAR_PIECES]
    pole_ref, residue_ref, reader_ref, src_ref, delay_ref, state_ref = rest[FAR_PIECES:][:6]
    far_ref, cur_ref, near_ref, exc_ref, sem = rest[FAR_PIECES + 6 :]
    size = far_ref.shape[0] // FAR_PIECES
    copies = fetch(
        sem,
        (reader_hbm, reader_ref),
        (src_hbm, src_ref),
        (delay_hbm, delay_ref),
        (pole_hbm, pole_ref),
        (residue_hbm, residue_ref),
        (state_hbm, state_ref),
        (cur_hbm, cur_ref),
        (near_hbm, near_ref),
        (exc_hbm, exc_ref),
        *(
            (far_hbm.at[pl.ds(n * size, size)], far_ref.at[pl.ds(n * size, size)])
            for n in range(FAR_PIECES)
        ),
    )
    reader_copy, src_copy, delay_copy, pole_copy, residue_copy, state_copy = copies[:6]
    cap, classes, groups = reader_ref.shape
    slots = cap * groups
    group_tiles = hits_ref.shape[0]
    slot = lax.broadcasted_iota(I32, (slots, 1), 0)
    row = lax.broadcasted_iota(I32, split_ref.shape[1:], 1)
    group_bits = groups.bit_length() - 1
    start = 4 * (slot & (groups - 1)) + shifted(slot, group_bits)
    for h in range(2):
        split_ref[h] = jnp.where(row == start + 2 * h, 1.0, 0.0).astype(BF16)
    reader_copy.wait()
    readers = jnp.concatenate([reader_ref[c] for c in range(cap)], axis=1)
    place = lax.broadcasted_iota(I32, (group_tiles, slots), 0)
    for k in range(classes):
        hits_ref[:, k * slots : (k + 1) * slots] = jnp.where(
            place == readers[k : k + 1], 1.0, 0.0
        ).astype(BF16)
    src_copy.wait()
    delay_copy.wait()
    sources, tiles = src_ref.shape
    near_row = ((delay_ref[...] - 1) * tiles + src_ref[...]).astype(F32).astype(BF16)
    eye = jnp.where(
        lax.broadcasted_iota(I32, (tiles, tiles), 0) == lax.broadcasted_iota(I32, (tiles, tiles), 1),
        1.0,
        0.0,
    ).astype(BF16)
    near_col = lax.dot_general(eye, near_row, CONTRACT_LAST, preferred_element_type=F32)
    near_col = near_col.astype(I32)
    at = lax.broadcasted_iota(I32, (tiles, near_pick_ref.shape[1]), 1)
    near_pick_ref[...] = jnp.concatenate(
        [jnp.where(at == near_col[:, a : a + 1], 1.0, 0.0) for a in range(sources)], axis=0
    ).astype(BF16)
    pole_copy.wait()
    residue_copy.wait()
    state_copy.wait()
    count = state_ref.shape[0]
    scale = [residue_ref[p] for p in range(count)]
    width = coef_ref.shape[1]
    for n in range(STEPS):
        total = scale[0]
        for p in range(1, count):
            total = total + scale[p]
        coef_ref[n : n + 1, :] = jnp.full((1, width), total, F32)
        if n + 1 < STEPS:
            scale = [scale[p] * pole_ref[p] for p in range(count)]
            tail = scale[0] * state_ref[0]
            for p in range(1, count):
                tail = tail + scale[p] * state_ref[p]
            tail_ref[n] = tail
    for p in range(count):
        coef_ref[8 + p : 9 + p, :] = jnp.full((1, width), pole_ref[p], F32)
    for n in range(6, 9):
        copies[n].wait()
    base_ref[...] = near_base(0, near_pick_ref, cur_ref, near_ref, exc_ref)
    for n in range(FAR_PIECES):
        copies[9 + n].wait()
        for k in range(size):
            turned[n][k] = far_ref[n * size + k].T


def far_terms(entries, turned, terms_ref):
    slots = entries.shape[0]
    at = 0
    for piece in turned:
        for k in range(piece.shape[0]):
            terms = lax.dot(entries, piece[k], preferred_element_type=F32)
            terms_ref[pl.ds(at, slots), :] = terms.astype(BF16)
            at += slots


def entries_of(in_ref, split_ref):
    incoming = in_ref[...]
    return jnp.concatenate(
        [
            lax.dot(split_ref[h], incoming, preferred_element_type=F32).astype(BF16)
            for h in range(2)
        ],
        axis=1,
    )


def near_base(step, near_pick_ref, cur_ref, near_ref, exc_ref):
    near_rows = lax.dot(near_pick_ref[...], cur_ref[...], preferred_element_type=F32).astype(BF16)
    classes = near_ref.shape[0]
    tiles = exc_ref.shape[1]
    per_class = near_rows.shape[0] // classes
    base = exc_ref[step].astype(F32)
    for k in range(classes):
        near = lax.dot_general(
            near_rows[k * per_class : (k + 1) * per_class],
            near_ref[k],
            CONTRACT_LAST,
            preferred_element_type=F32,
        )
        for m in range(per_class // tiles):
            base = base - near[m * tiles : (m + 1) * tiles]
    return base


def far_first_kernel(in_ref, split_ref, hits_ref, *rest):
    *turned, part_ref, terms_ref = rest
    far_terms(entries_of(in_ref, split_ref), turned, terms_ref)
    part_ref[...] = lax.dot(
        hits_ref[...], terms_ref[...], preferred_element_type=F32
    ).astype(BF16)


def far_kernel(step, in_ref, split_ref, hits_ref, *rest):
    *turned, near_pick_ref, cur_ref, near_ref, exc_ref, part_ref, base_ref, terms_ref = rest
    far_terms(entries_of(in_ref, split_ref), turned, terms_ref)
    base_ref[...] = near_base(step, near_pick_ref, cur_ref, near_ref, exc_ref)
    part_ref[...] = lax.dot(
        hits_ref[...], terms_ref[...], preferred_element_type=F32
    ).astype(BF16)


def solve(parts_ref, base_ref, inverse_ref, turned_ref=None):
    far_field = parts_ref[0].astype(F32)
    for o in range(1, parts_ref.shape[0]):
        far_field = far_field + parts_ref[o].astype(F32)
    right_side = (base_ref[...] - far_field).astype(BF16)
    tiles = right_side.shape[0]
    row = lax.broadcasted_iota(I32, right_side.shape, 0)
    current = jnp.zeros(right_side.shape, F32)
    for t in range(tiles):
        turned = inverse_ref[t]
        if turned_ref is not None:
            turned = turned.T
            turned_ref[t] = turned
        current = jnp.where(
            row == t, lax.dot(right_side, turned, preferred_element_type=F32), current
        )
    return current.astype(BF16)


def step_kernel(
    step, coef_ref, parts_ref, base_ref, inverse_ref, tail_ref, cur_ref, ret_ref, pick_ref,
    cur_out, send_ref, ret_out=None, turned_ref=None,
):
    current = solve(parts_ref, base_ref, inverse_ref, turned_ref)
    tiles = current.shape[0]
    wide = current.astype(F32)
    retarded = wide * (1.0 + coef_ref[0:1, :]) + tail_ref[step]
    for back in range(1, step + 1):
        past = cur_ref[pl.ds((back - 1) * tiles, tiles), :]
        retarded = retarded + coef_ref[back : back + 1, :] * past.astype(F32)
    kept = cur_ref.shape[0] - tiles
    cur_out[...] = jnp.concatenate([current, cur_ref[:kept, :]], axis=0)
    history = jnp.concatenate([retarded.astype(BF16), ret_ref[:kept, :]], axis=0)
    if ret_out is not None:
        ret_out[...] = history
    send_ref[...] = lax.dot(
        pick_ref[...], halves_stacked(history), preferred_element_type=F32
    ).astype(BF16)


def last_kernel(coef_ref, parts_ref, base_ref, inverse_ref, cur_ref, state_ref, cur_out, state_out):
    current = solve(parts_ref, base_ref, inverse_ref)
    tiles = current.shape[0]
    past = [cur_ref[pl.ds((STEPS - 2 - n) * tiles, tiles), :] for n in range(STEPS - 1)] + [current]
    for n in range(STEPS):
        cur_out[n] = past[n]
    wide = [c.astype(F32) for c in past]
    for p in range(state_ref.shape[0]):
        pole = coef_ref[8 + p : 9 + p, :]
        state = state_ref[p]
        for n in range(STEPS):
            state = pole * state + wide[n]
        state_out[p] = state


def in_hbm(x):
    return pltpu.with_memory_space_constraint(x, pltpu.HBM)


def call(kernel, name, outs, specs, scratch=()):
    return pl.pallas_call(
        kernel,
        name=name,
        out_shape=outs,
        in_specs=specs,
        out_specs=jax.tree.map(lambda _: VMEM, outs),
        scratch_shapes=scratch,
        compiler_params=pltpu.CompilerParams(vmem_limit_bytes=8 << 20),
    )


def body(
    excitation,
    cur_hist,
    ret_hist,
    pole_state,
    self_inverse,
    near_mats,
    far_mats,
    poles,
    residues,
    near_src,
    near_delay,
    far_dest,
    far_delay,
    far_reader,
):
    groups = far_reader.shape[1]
    cap = far_reader.shape[3]
    classes = far_reader.shape[4]
    tiles = excitation.shape[1]
    width = excitation.shape[2]
    owners = lax.axis_size("own")
    group_tiles = tiles * owners
    slots = groups * cap
    past = HIST * tiles
    shape = jax.ShapeDtypeStruct

    history = ret_hist.reshape(past, width)
    names = far_dest.shape[1]
    pick, outgoing = call(
        first_kernel,
        "first",
        (shape((2 * slots, 2 * past), BF16), shape((2 * slots, LANES), BF16)),
        [HBM] * 3,
        [
            pltpu.VMEM((names, tiles), I32),
            pltpu.VMEM((names, tiles), I32),
            pltpu.VMEM((past, width), BF16),
            pltpu.SemaphoreType.DMA((3,)),
        ],
    )(in_hbm(far_dest.T), in_hbm(far_delay.T), in_hbm(history))

    current = cur_hist.reshape(past, width)
    sources = near_src.shape[0] * near_src.shape[2]
    poles_count = poles.shape[0]
    reader_hits, split, near_pick, tail, coef, base, *turned = call(
        tables_kernel,
        "tables",
        (
            shape((group_tiles, classes * slots), BF16),
            shape((2, slots, 2 * slots), BF16),
            shape((sources * tiles, past), BF16),
            shape((STEPS - 1, tiles, width), F32),
            shape((8 + poles_count, width), F32),
            shape((tiles, width), F32),
            *[shape((classes // FAR_PIECES, width, width), BF16)] * FAR_PIECES,
        ),
        [HBM] * 10,
        [
            pltpu.SMEM((poles_count,), F32),
            pltpu.SMEM((poles_count,), F32),
            pltpu.VMEM((cap, classes, groups), I32),
            pltpu.VMEM((sources, tiles), I32),
            pltpu.VMEM((sources, tiles), I32),
            pltpu.VMEM(pole_state.shape, F32),
            pltpu.VMEM(far_mats.shape, BF16),
            pltpu.VMEM((past, width), BF16),
            pltpu.VMEM(near_mats.shape, BF16),
            pltpu.VMEM(excitation.shape, BF16),
            pltpu.SemaphoreType.DMA((9 + FAR_PIECES,)),
        ],
    )(
        in_hbm(poles),
        in_hbm(residues),
        in_hbm(far_reader[0, :, 0].transpose(1, 2, 0)),
        in_hbm(near_src.transpose(0, 2, 1).reshape(sources, tiles)),
        in_hbm(near_delay.transpose(0, 2, 1).reshape(sources, tiles)),
        in_hbm(pole_state),
        in_hbm(far_mats),
        in_hbm(current),
        in_hbm(near_mats),
        in_hbm(excitation),
    )

    inverse = self_inverse
    retarded = history
    for step in range(STEPS):
        incoming = lax.all_to_all(
            outgoing.reshape(groups, 2 * cap, LANES), "grp", split_axis=0, concat_axis=0, tiled=True
        ).reshape(2 * slots, LANES)
        if step == 0:
            incoming, tail, coef, base, reader_hits, near_pick, split, *turned = (
                lax.optimization_barrier(
                    (incoming, tail, coef, base, reader_hits, near_pick, split, *turned)
                )
            )
        sums = shape((group_tiles, width), BF16)
        terms = pltpu.VMEM((classes * slots, width), BF16)
        kept = (incoming, split, reader_hits, *turned)
        if step == 0:
            part = call(far_first_kernel, "far", sums, [VMEM] * len(kept), [terms])(*kept)
        else:
            part, base = call(
                functools.partial(far_kernel, step),
                "far",
                (sums, shape((tiles, width), F32)),
                [VMEM] * (len(kept) + 4),
                [terms],
            )(*kept, near_pick, current, near_mats, excitation)
        parts = lax.all_to_all(
            part.reshape(owners, tiles, width), "own", split_axis=0, concat_axis=0, tiled=True
        )
        if step + 1 < STEPS:
            outs = (shape((past, width), BF16), shape((2 * slots, LANES), BF16))
            if step + 2 < STEPS:
                outs = outs + (shape((past, width), BF16),)
            if step == 0:
                outs = outs + (shape(self_inverse.shape, BF16),)
            made = call(functools.partial(step_kernel, step), "step", outs, [VMEM] * 8)(
                coef, parts, base, inverse, tail, current, retarded, pick
            )
            current, outgoing = made[:2]
            if step + 2 < STEPS:
                retarded = made[2]
            if step == 0:
                inverse = made[3]
    return call(
        last_kernel,
        "last",
        (shape((STEPS, tiles, width), BF16), shape(pole_state.shape, F32)),
        [VMEM] * 6,
    )(coef, parts, base, inverse, current, pole_state)


def solution(mesh):
    in_specs = (
        P(None, ("grp", "own"), None),
        P(None, ("grp", "own"), None),
        P(None, ("grp", "own"), None),
        P(None, ("grp", "own"), None),
        P(("grp", "own"), None, None),
        P(),
        P(),
        P(),
        P(),
        P(None, ("grp", "own"), None),
        P(None, ("grp", "own"), None),
        P(("grp", "own"), None),
        P(("grp", "own"), None),
        P("grp", None, "own", None, None),
    )
    out_specs = (P(None, ("grp", "own"), None), P(None, ("grp", "own"), None))
    return jax.shard_map(body, mesh=mesh, in_specs=in_specs, out_specs=out_specs, check_vma=False)
```

```python
import functools

import jax
import jax.numpy as jnp
from jax import lax
from jax.experimental import pallas as pl
from jax.experimental.pallas import tpu as pltpu
from jax.sharding import PartitionSpec as P

STEPS = 4
HIST = 4
F32 = jnp.float32
BF16 = jnp.bfloat16
I32 = jnp.int32
LANES = 128
FAR_PIECES = 4
OUT_PIECES = 2
CONTRACT_LAST = (((1,), (1,)), ((), ()))
VMEM = pl.BlockSpec(memory_space=pltpu.VMEM)
HBM = pl.BlockSpec(memory_space=pltpu.HBM)


def halves_stacked(rows):
    return jnp.concatenate([rows[:, :LANES], rows[:, LANES:]], axis=0)


def shifted(x, bits):
    return lax.shift_right_logical(x, jnp.full(x.shape, bits, x.dtype))


def fetch(sem, *pairs):
    copies = [pltpu.make_async_copy(src, dst, sem.at[n]) for n, (src, dst) in enumerate(pairs)]
    for copy in copies:
        copy.start()
    return copies


def first_kernel(
    dest_hbm, delay_hbm, ret_hbm, pick_ref, out_ref, dest_ref, delay_ref, ret_ref, sem
):
    copies = fetch(sem, (dest_hbm, dest_ref), (delay_hbm, delay_ref), (ret_hbm, ret_ref))
    names, tiles = dest_ref.shape
    shape = pick_ref.shape
    rows, cols = shape
    at = lax.broadcasted_iota(I32, shape, 0)
    col = lax.broadcasted_iota(I32, (1, cols), 1)
    tile_bits = tiles.bit_length() - 1
    group = shifted(at, 2)
    slab = shifted(col, tile_bits)
    col_delay = (slab & (HIST - 1)) + 1
    col_half = shifted(col, tile_bits + HIST.bit_length() - 1)
    spread = jnp.where(
        lax.broadcasted_iota(I32, (tiles, cols), 0) == (col & (tiles - 1)), 1.0, 0.0
    ).astype(BF16)
    of = lax.broadcasted_iota(I32, (cols, cols), 0)
    earlier = jnp.where((shifted(of, tile_bits) == slab) & (of < col), 1.0, 0.0).astype(BF16)
    placed = (col_half == (shifted(at, 1) & 1)).astype(F32)
    rank = (at & 1).astype(F32)
    copies[0].wait()
    copies[1].wait()
    dest = lax.dot(dest_ref[...].astype(F32).astype(BF16), spread, preferred_element_type=F32)
    delay = lax.dot(delay_ref[...].astype(F32).astype(BF16), spread, preferred_element_type=F32)
    dest = dest.astype(I32)
    on_time = delay.astype(I32) == col_delay
    dest_on_time = jnp.where(on_time, dest, -1)
    named = jnp.zeros(shape, F32)
    timed = jnp.zeros(shape, F32)
    for j in range(names):
        named = jnp.where(dest[j : j + 1] == group, 1.0, named)
        timed = jnp.where(dest_on_time[j : j + 1] == group, placed, timed)
    before = lax.dot(named.astype(BF16), earlier, preferred_element_type=F32)
    pick = jnp.where(before == rank, timed, 0.0).astype(BF16)
    pick_ref[...] = pick
    copies[2].wait()
    out_ref[...] = lax.dot(
        pick, halves_stacked(ret_ref[...]), preferred_element_type=F32
    ).astype(BF16)


def tables_kernel(
    pole_hbm, residue_hbm, reader_hbm, src_hbm, delay_hbm, state_hbm, far_hbm,
    cur_hbm, near_hbm, exc_hbm, hits_ref, split_ref, near_pick_ref, tail_ref, coef_ref, base_ref,
    near_ref, *rest,
):
    turned = rest[:FAR_PIECES]
    pole_ref, residue_ref, reader_ref, src_ref, delay_ref, state_ref = rest[FAR_PIECES:][:6]
    far_ref, cur_ref, near_in_ref, exc_ref, sem = rest[FAR_PIECES + 6 :]
    size = far_ref.shape[0] // FAR_PIECES
    copies = fetch(
        sem,
        (reader_hbm, reader_ref),
        (src_hbm, src_ref),
        (delay_hbm, delay_ref),
        (pole_hbm, pole_ref),
        (residue_hbm, residue_ref),
        (state_hbm, state_ref),
        (cur_hbm, cur_ref),
        (near_hbm, near_in_ref),
        (exc_hbm, exc_ref),
        *(
            (far_hbm.at[pl.ds(n * size, size)], far_ref.at[pl.ds(n * size, size)])
            for n in range(FAR_PIECES)
        ),
    )
    reader_copy, src_copy, delay_copy, pole_copy, residue_copy, state_copy = copies[:6]
    cap, classes, groups = reader_ref.shape
    slots = cap * groups
    group_tiles = hits_ref.shape[0]
    slot = lax.broadcasted_iota(I32, (slots, 1), 0)
    row = lax.broadcasted_iota(I32, (slots, 2 * slots), 1)
    group_bits = groups.bit_length() - 1
    start = 4 * (slot & (groups - 1)) + shifted(slot, group_bits)
    for h in range(2):
        split_ref[h * slots : (h + 1) * slots, :] = jnp.where(
            row == start + 2 * h, 1.0, 0.0
        ).astype(BF16)
    reader_copy.wait()
    readers = jnp.concatenate([reader_ref[c] for c in range(cap)], axis=1)
    place = lax.broadcasted_iota(I32, (group_tiles, slots), 0)
    for k in range(classes):
        hits_ref[:, k * slots : (k + 1) * slots] = jnp.where(
            place == readers[k : k + 1], 1.0, 0.0
        ).astype(BF16)
    src_copy.wait()
    delay_copy.wait()
    sources, tiles = src_ref.shape
    near_row = ((delay_ref[...] - 1) * tiles + src_ref[...]).astype(F32).astype(BF16)
    eye = jnp.where(
        lax.broadcasted_iota(I32, (tiles, tiles), 0) == lax.broadcasted_iota(I32, (tiles, tiles), 1),
        1.0,
        0.0,
    ).astype(BF16)
    near_col = lax.dot_general(eye, near_row, CONTRACT_LAST, preferred_element_type=F32)
    near_col = near_col.astype(I32)
    at = lax.broadcasted_iota(I32, (tiles, near_pick_ref.shape[1]), 1)
    near_pick_ref[...] = jnp.concatenate(
        [jnp.where(at == near_col[:, a : a + 1], 1.0, 0.0) for a in range(sources)], axis=0
    ).astype(BF16)
    pole_copy.wait()
    residue_copy.wait()
    state_copy.wait()
    count = state_ref.shape[0]
    scale = [residue_ref[p] for p in range(count)]
    width = coef_ref.shape[1]
    for n in range(STEPS):
        total = scale[0]
        for p in range(1, count):
            total = total + scale[p]
        coef_ref[n : n + 1, :] = jnp.full((1, width), total, F32)
        if n + 1 < STEPS:
            scale = [scale[p] * pole_ref[p] for p in range(count)]
            tail = scale[0] * state_ref[0]
            for p in range(1, count):
                tail = tail + scale[p] * state_ref[p]
            tail_ref[n] = tail
    for p in range(count):
        coef_ref[8 + p : 9 + p, :] = jnp.full((1, width), pole_ref[p], F32)
    for n in range(6, 9):
        copies[n].wait()
    for k in range(near_ref.shape[0]):
        near_ref[k] = near_in_ref[k].T
    base_ref[...] = near_base(0, near_pick_ref, cur_ref, near_ref, exc_ref)
    for n in range(FAR_PIECES):
        copies[9 + n].wait()
        for k in range(size):
            turned[n][k] = far_ref[n * size + k].T


def far_terms(entries, turned, terms_ref):
    slots = entries.shape[0]
    at = 0
    for piece in turned:
        for k in range(piece.shape[0]):
            terms = lax.dot(entries, piece[k], preferred_element_type=F32)
            terms_ref[pl.ds(at, slots), :] = terms.astype(BF16)
            at += slots


def entries_of(in_ref, split_ref):
    halves = lax.dot(split_ref[...], in_ref[...], preferred_element_type=F32).astype(BF16)
    slots = halves.shape[0] // 2
    return jnp.concatenate([halves[:slots], halves[slots:]], axis=1)


def near_base(step, near_pick_ref, cur_ref, near_ref, exc_ref):
    near_rows = lax.dot(near_pick_ref[...], cur_ref[...], preferred_element_type=F32).astype(BF16)
    classes = near_ref.shape[0]
    tiles = exc_ref.shape[1]
    per_class = near_rows.shape[0] // classes
    base = exc_ref[step].astype(F32)
    for k in range(classes):
        near = lax.dot(
            near_rows[k * per_class : (k + 1) * per_class],
            near_ref[k],
            preferred_element_type=F32,
        )
        for m in range(per_class // tiles):
            base = base - near[m * tiles : (m + 1) * tiles]
    return base


def far_first_kernel(in_ref, split_ref, hits_ref, *rest):
    *turned, part_ref, terms_ref = rest
    far_terms(entries_of(in_ref, split_ref), turned, terms_ref)
    part_ref[...] = lax.dot(
        hits_ref[...], terms_ref[...], preferred_element_type=F32
    ).astype(BF16)


def far_kernel(step, in_ref, split_ref, hits_ref, *rest):
    *turned, near_pick_ref, cur_ref, near_ref, exc_ref, part_ref, base_ref, terms_ref = rest
    far_terms(entries_of(in_ref, split_ref), turned, terms_ref)
    base_ref[...] = near_base(step, near_pick_ref, cur_ref, near_ref, exc_ref)
    part_ref[...] = lax.dot(
        hits_ref[...], terms_ref[...], preferred_element_type=F32
    ).astype(BF16)


def solve(parts_ref, base_ref, inverse_ref, turned_ref=None):
    far_field = parts_ref[0].astype(F32)
    for o in range(1, parts_ref.shape[0]):
        far_field = far_field + parts_ref[o].astype(F32)
    right_side = (base_ref[...] - far_field).astype(BF16)
    tiles = right_side.shape[0]
    row = lax.broadcasted_iota(I32, right_side.shape, 0)
    current = jnp.zeros(right_side.shape, F32)
    for t in range(tiles):
        turned = inverse_ref[t]
        if turned_ref is not None:
            turned = turned.T
            turned_ref[t] = turned
        current = jnp.where(
            row == t, lax.dot(right_side, turned, preferred_element_type=F32), current
        )
    return current.astype(BF16)


def step_kernel(
    step, coef_ref, parts_ref, base_ref, inverse_ref, tail_ref, cur_ref, ret_ref, pick_ref,
    cur_out, send_ref, ret_out=None, turned_ref=None,
):
    current = solve(parts_ref, base_ref, inverse_ref, turned_ref)
    tiles = current.shape[0]
    wide = current.astype(F32)
    retarded = wide * (1.0 + coef_ref[0:1, :]) + tail_ref[step]
    for back in range(1, step + 1):
        past = cur_ref[pl.ds((back - 1) * tiles, tiles), :]
        retarded = retarded + coef_ref[back : back + 1, :] * past.astype(F32)
    kept = cur_ref.shape[0] - tiles
    cur_out[...] = jnp.concatenate([current, cur_ref[:kept, :]], axis=0)
    history = jnp.concatenate([retarded.astype(BF16), ret_ref[:kept, :]], axis=0)
    if ret_out is not None:
        ret_out[...] = history
    send_ref[...] = lax.dot(
        pick_ref[...], halves_stacked(history), preferred_element_type=F32
    ).astype(BF16)


def last_kernel(
    coef_ref, parts_ref, base_ref, inverse_ref, cur_ref, state_ref, cur_out, state_out,
    now_ref, made_ref, sem,
):
    tiles = now_ref.shape[0]
    olds = [cur_ref.at[pl.ds((STEPS - 2 - n) * tiles, tiles)] for n in range(STEPS - 1)]
    copies = fetch(sem, *((old, cur_out.at[n]) for n, old in enumerate(olds)))
    current = solve(parts_ref, base_ref, inverse_ref)
    now_ref[...] = current
    copies.append(pltpu.make_async_copy(now_ref, cur_out.at[STEPS - 1], sem.at[STEPS - 1]))
    copies[-1].start()
    wide = [old[...].astype(F32) for old in olds] + [current.astype(F32)]
    size = state_ref.shape[0] // OUT_PIECES
    for piece in range(OUT_PIECES):
        for p in range(piece * size, (piece + 1) * size):
            pole = coef_ref[8 + p : 9 + p, :]
            state = state_ref[p]
            for n in range(STEPS):
                state = pole * state + wide[n]
            made_ref[p] = state
        rows = pl.ds(piece * size, size)
        copies.append(
            pltpu.make_async_copy(made_ref.at[rows], state_out.at[rows], sem.at[STEPS + piece])
        )
        copies[-1].start()
    for copy in copies:
        copy.wait()


def in_hbm(x):
    return pltpu.with_memory_space_constraint(x, pltpu.HBM)


def call(kernel, name, outs, specs, scratch=(), out_spec=VMEM):
    return pl.pallas_call(
        kernel,
        name=name,
        out_shape=outs,
        in_specs=specs,
        out_specs=jax.tree.map(lambda _: out_spec, outs),
        scratch_shapes=scratch,
        compiler_params=pltpu.CompilerParams(vmem_limit_bytes=8 << 20),
    )


def body(
    excitation,
    cur_hist,
    ret_hist,
    pole_state,
    self_inverse,
    near_mats,
    far_mats,
    poles,
    residues,
    near_src,
    near_delay,
    far_dest,
    far_delay,
    far_reader,
):
    groups = far_reader.shape[1]
    cap = far_reader.shape[3]
    classes = far_reader.shape[4]
    tiles = excitation.shape[1]
    width = excitation.shape[2]
    owners = lax.axis_size("own")
    group_tiles = tiles * owners
    slots = groups * cap
    past = HIST * tiles
    shape = jax.ShapeDtypeStruct

    history = ret_hist.reshape(past, width)
    names = far_dest.shape[1]
    pick, outgoing = call(
        first_kernel,
        "first",
        (shape((2 * slots, 2 * past), BF16), shape((2 * slots, LANES), BF16)),
        [HBM] * 3,
        [
            pltpu.VMEM((names, tiles), I32),
            pltpu.VMEM((names, tiles), I32),
            pltpu.VMEM((past, width), BF16),
            pltpu.SemaphoreType.DMA((3,)),
        ],
    )(in_hbm(far_dest.T), in_hbm(far_delay.T), in_hbm(history))

    current = cur_hist.reshape(past, width)
    sources = near_src.shape[0] * near_src.shape[2]
    poles_count = poles.shape[0]
    reader_hits, split, near_pick, tail, coef, base, near, *turned = call(
        tables_kernel,
        "tables",
        (
            shape((group_tiles, classes * slots), BF16),
            shape((2 * slots, 2 * slots), BF16),
            shape((sources * tiles, past), BF16),
            shape((STEPS - 1, tiles, width), F32),
            shape((8 + poles_count, width), F32),
            shape((tiles, width), F32),
            shape(near_mats.shape, BF16),
            *[shape((classes // FAR_PIECES, width, width), BF16)] * FAR_PIECES,
        ),
        [HBM] * 10,
        [
            pltpu.SMEM((poles_count,), F32),
            pltpu.SMEM((poles_count,), F32),
            pltpu.VMEM((cap, classes, groups), I32),
            pltpu.VMEM((sources, tiles), I32),
            pltpu.VMEM((sources, tiles), I32),
            pltpu.VMEM(pole_state.shape, F32),
            pltpu.VMEM(far_mats.shape, BF16),
            pltpu.VMEM((past, width), BF16),
            pltpu.VMEM(near_mats.shape, BF16),
            pltpu.VMEM(excitation.shape, BF16),
            pltpu.SemaphoreType.DMA((9 + FAR_PIECES,)),
        ],
    )(
        in_hbm(poles),
        in_hbm(residues),
        in_hbm(far_reader[0, :, 0].transpose(1, 2, 0)),
        in_hbm(near_src.transpose(0, 2, 1).reshape(sources, tiles)),
        in_hbm(near_delay.transpose(0, 2, 1).reshape(sources, tiles)),
        in_hbm(pole_state),
        in_hbm(far_mats),
        in_hbm(current),
        in_hbm(near_mats),
        in_hbm(excitation),
    )

    inverse = self_inverse
    retarded = history
    for step in range(STEPS):
        incoming = lax.all_to_all(
            outgoing.reshape(groups, 2 * cap, LANES), "grp", split_axis=0, concat_axis=0, tiled=True
        ).reshape(2 * slots, LANES)
        if step == 0:
            incoming, tail, coef, base, near, reader_hits, near_pick, split, *turned = (
                lax.optimization_barrier(
                    (incoming, tail, coef, base, near, reader_hits, near_pick, split, *turned)
                )
            )
        sums = shape((group_tiles, width), BF16)
        terms = pltpu.VMEM((classes * slots, width), BF16)
        kept = (incoming, split, reader_hits, *turned)
        if step == 0:
            part = call(far_first_kernel, "far", sums, [VMEM] * len(kept), [terms])(*kept)
        else:
            part, base = call(
                functools.partial(far_kernel, step),
                "far",
                (sums, shape((tiles, width), F32)),
                [VMEM] * (len(kept) + 4),
                [terms],
            )(*kept, near_pick, current, near, excitation)
        parts = lax.all_to_all(
            part.reshape(owners, tiles, width), "own", split_axis=0, concat_axis=0, tiled=True
        )
        if step + 1 < STEPS:
            outs = (shape((past, width), BF16), shape((2 * slots, LANES), BF16))
            if step + 2 < STEPS:
                outs = outs + (shape((past, width), BF16),)
            if step == 0:
                outs = outs + (shape(self_inverse.shape, BF16),)
            made = call(functools.partial(step_kernel, step), "step", outs, [VMEM] * 8)(
                coef, parts, base, inverse, tail, current, retarded, pick
            )
            current, outgoing = made[:2]
            if step + 2 < STEPS:
                retarded = made[2]
            if step == 0:
                inverse = made[3]
    return call(
        last_kernel,
        "last",
        (shape((STEPS, tiles, width), BF16), shape(pole_state.shape, F32)),
        [VMEM] * 6,
        [
            pltpu.VMEM((tiles, width), BF16),
            pltpu.VMEM(pole_state.shape, F32),
            pltpu.SemaphoreType.DMA((STEPS + OUT_PIECES,)),
        ],
        HBM,
    )(coef, parts, base, inverse, current, pole_state)


def solution(mesh):
    in_specs = (
        P(None, ("grp", "own"), None),
        P(None, ("grp", "own"), None),
        P(None, ("grp", "own"), None),
        P(None, ("grp", "own"), None),
        P(("grp", "own"), None, None),
        P(),
        P(),
        P(),
        P(),
        P(None, ("grp", "own"), None),
        P(None, ("grp", "own"), None),
        P(("grp", "own"), None),
        P(("grp", "own"), None),
        P("grp", None, "own", None, None),
    )
    out_specs = (P(None, ("grp", "own"), None), P(None, ("grp", "own"), None))
    return jax.shard_map(body, mesh=mesh, in_specs=in_specs, out_specs=out_specs, check_vma=False)
```

```python
import functools

import jax
import jax.numpy as jnp
from jax import lax
from jax.experimental import pallas as pl
from jax.experimental.pallas import tpu as pltpu
from jax.sharding import PartitionSpec as P

STEPS = 4
HIST = 4
F32 = jnp.float32
BF16 = jnp.bfloat16
I32 = jnp.int32
LANES = 128
FAR_PIECES = 4
CONTRACT_LAST = (((1,), (1,)), ((), ()))
VMEM = pl.BlockSpec(memory_space=pltpu.VMEM)
HBM = pl.BlockSpec(memory_space=pltpu.HBM)


def halves_stacked(rows):
    return jnp.concatenate([rows[:, :LANES], rows[:, LANES:]], axis=0)


def shifted(x, bits):
    return lax.shift_right_logical(x, jnp.full(x.shape, bits, x.dtype))


def fetch(sem, *pairs):
    copies = [pltpu.make_async_copy(src, dst, sem.at[n]) for n, (src, dst) in enumerate(pairs)]
    for copy in copies:
        copy.start()
    return copies


def first_kernel(
    dest_hbm, delay_hbm, ret_hbm, pick_ref, out_ref, dest_ref, delay_ref, ret_ref, sem
):
    copies = fetch(sem, (dest_hbm, dest_ref), (delay_hbm, delay_ref), (ret_hbm, ret_ref))
    names, tiles = dest_ref.shape
    shape = pick_ref.shape
    rows, cols = shape
    at = lax.broadcasted_iota(I32, shape, 0)
    col = lax.broadcasted_iota(I32, (1, cols), 1)
    tile_bits = tiles.bit_length() - 1
    group = shifted(at, 2)
    slab = shifted(col, tile_bits)
    col_delay = (slab & (HIST - 1)) + 1
    col_half = shifted(col, tile_bits + HIST.bit_length() - 1)
    spread = jnp.where(
        lax.broadcasted_iota(I32, (tiles, cols), 0) == (col & (tiles - 1)), 1.0, 0.0
    ).astype(BF16)
    of = lax.broadcasted_iota(I32, (cols, cols), 0)
    earlier = jnp.where((shifted(of, tile_bits) == slab) & (of < col), 1.0, 0.0).astype(BF16)
    placed = (col_half == (shifted(at, 1) & 1)).astype(F32)
    rank = (at & 1).astype(F32)
    copies[0].wait()
    copies[1].wait()
    dest = lax.dot(dest_ref[...].astype(F32).astype(BF16), spread, preferred_element_type=F32)
    delay = lax.dot(delay_ref[...].astype(F32).astype(BF16), spread, preferred_element_type=F32)
    dest = dest.astype(I32)
    on_time = delay.astype(I32) == col_delay
    dest_on_time = jnp.where(on_time, dest, -1)
    named = jnp.zeros(shape, F32)
    timed = jnp.zeros(shape, F32)
    for j in range(names):
        named = jnp.where(dest[j : j + 1] == group, 1.0, named)
        timed = jnp.where(dest_on_time[j : j + 1] == group, placed, timed)
    before = lax.dot(named.astype(BF16), earlier, preferred_element_type=F32)
    pick = jnp.where(before == rank, timed, 0.0).astype(BF16)
    pick_ref[...] = pick
    copies[2].wait()
    out_ref[...] = lax.dot(
        pick, halves_stacked(ret_ref[...]), preferred_element_type=F32
    ).astype(BF16)


def tables_kernel(
    pole_hbm, residue_hbm, reader_hbm, src_hbm, delay_hbm, state_hbm, far_hbm,
    cur_hbm, near_hbm, exc_hbm, hits_ref, split_ref, near_pick_ref, tail_ref, coef_ref, base_ref,
    *rest,
):
    turned = rest[:FAR_PIECES]
    pole_ref, residue_ref, reader_ref, src_ref, delay_ref, state_ref = rest[FAR_PIECES:][:6]
    far_ref, cur_ref, near_ref, exc_ref, sem = rest[FAR_PIECES + 6 :]
    size = far_ref.shape[0] // FAR_PIECES
    copies = fetch(
        sem,
        (reader_hbm, reader_ref),
        (src_hbm, src_ref),
        (delay_hbm, delay_ref),
        (pole_hbm, pole_ref),
        (residue_hbm, residue_ref),
        (state_hbm, state_ref),
        (cur_hbm, cur_ref),
        (near_hbm, near_ref),
        (exc_hbm, exc_ref),
        *(
            (far_hbm.at[pl.ds(n * size, size)], far_ref.at[pl.ds(n * size, size)])
            for n in range(FAR_PIECES)
        ),
    )
    reader_copy, src_copy, delay_copy, pole_copy, residue_copy, state_copy = copies[:6]
    cap, classes, groups = reader_ref.shape
    slots = cap * groups
    group_tiles = hits_ref.shape[0]
    slot = lax.broadcasted_iota(I32, (slots, 1), 0)
    row = lax.broadcasted_iota(I32, (slots, 2 * slots), 1)
    group_bits = groups.bit_length() - 1
    start = 4 * (slot & (groups - 1)) + shifted(slot, group_bits)
    for h in range(2):
        split_ref[h * slots : (h + 1) * slots, :] = jnp.where(
            row == start + 2 * h, 1.0, 0.0
        ).astype(BF16)
    reader_copy.wait()
    readers = jnp.concatenate([reader_ref[c] for c in range(cap)], axis=1)
    place = lax.broadcasted_iota(I32, (group_tiles, slots), 0)
    for k in range(classes):
        hits_ref[:, k * slots : (k + 1) * slots] = jnp.where(
            place == readers[k : k + 1], 1.0, 0.0
        ).astype(BF16)
    src_copy.wait()
    delay_copy.wait()
    sources, tiles = src_ref.shape
    near_row = ((delay_ref[...] - 1) * tiles + src_ref[...]).astype(F32).astype(BF16)
    eye = jnp.where(
        lax.broadcasted_iota(I32, (tiles, tiles), 0) == lax.broadcasted_iota(I32, (tiles, tiles), 1),
        1.0,
        0.0,
    ).astype(BF16)
    near_col = lax.dot_general(eye, near_row, CONTRACT_LAST, preferred_element_type=F32)
    near_col = near_col.astype(I32)
    at = lax.broadcasted_iota(I32, (tiles, near_pick_ref.shape[1]), 1)
    near_pick_ref[...] = jnp.concatenate(
        [jnp.where(at == near_col[:, a : a + 1], 1.0, 0.0) for a in range(sources)], axis=0
    ).astype(BF16)
    pole_copy.wait()
    residue_copy.wait()
    state_copy.wait()
    count = state_ref.shape[0]
    scale = [residue_ref[p] for p in range(count)]
    width = coef_ref.shape[1]
    for n in range(STEPS):
        total = scale[0]
        for p in range(1, count):
            total = total + scale[p]
        coef_ref[n : n + 1, :] = jnp.full((1, width), total, F32)
        if n + 1 < STEPS:
            scale = [scale[p] * pole_ref[p] for p in range(count)]
            tail = scale[0] * state_ref[0]
            for p in range(1, count):
                tail = tail + scale[p] * state_ref[p]
            tail_ref[n] = tail
    for p in range(count):
        coef_ref[8 + p : 9 + p, :] = jnp.full((1, width), pole_ref[p], F32)
    for n in range(6, 9):
        copies[n].wait()
    base_ref[...] = near_base(0, near_pick_ref, cur_ref, near_ref, exc_ref)
    for n in range(FAR_PIECES):
        copies[9 + n].wait()
        for k in range(size):
            turned[n][k] = far_ref[n * size + k].T


def far_terms(entries, turned, terms_ref):
    slots = entries.shape[0]
    at = 0
    for piece in turned:
        for k in range(piece.shape[0]):
            terms = lax.dot(entries, piece[k], preferred_element_type=F32)
            terms_ref[pl.ds(at, slots), :] = terms.astype(BF16)
            at += slots


def entries_of(in_ref, split_ref):
    halves = lax.dot(split_ref[...], in_ref[...], preferred_element_type=F32).astype(BF16)
    slots = halves.shape[0] // 2
    return jnp.concatenate([halves[:slots], halves[slots:]], axis=1)


def near_base(step, near_pick_ref, cur_ref, near_ref, exc_ref):
    near_rows = lax.dot(near_pick_ref[...], cur_ref[...], preferred_element_type=F32).astype(BF16)
    classes = near_ref.shape[0]
    tiles = exc_ref.shape[1]
    per_class = near_rows.shape[0] // classes
    base = exc_ref[step].astype(F32)
    for k in range(classes):
        near = lax.dot_general(
            near_rows[k * per_class : (k + 1) * per_class],
            near_ref[k],
            CONTRACT_LAST,
            preferred_element_type=F32,
        )
        for m in range(per_class // tiles):
            base = base - near[m * tiles : (m + 1) * tiles]
    return base


def far_first_kernel(in_ref, split_ref, hits_ref, *rest):
    *turned, part_ref, terms_ref = rest
    far_terms(entries_of(in_ref, split_ref), turned, terms_ref)
    part_ref[...] = lax.dot(
        hits_ref[...], terms_ref[...], preferred_element_type=F32
    ).astype(BF16)


def far_kernel(step, in_ref, split_ref, hits_ref, *rest):
    *turned, near_pick_ref, cur_ref, near_ref, exc_ref, part_ref, base_ref, terms_ref = rest
    entries = entries_of(in_ref, split_ref)
    base_ref[...] = near_base(step, near_pick_ref, cur_ref, near_ref, exc_ref)
    far_terms(entries, turned, terms_ref)
    part_ref[...] = lax.dot(
        hits_ref[...], terms_ref[...], preferred_element_type=F32
    ).astype(BF16)


def solve(parts_ref, base_ref, inverse_ref, turned_ref=None):
    far_field = parts_ref[0].astype(F32)
    for o in range(1, parts_ref.shape[0]):
        far_field = far_field + parts_ref[o].astype(F32)
    right_side = (base_ref[...] - far_field).astype(BF16)
    tiles = right_side.shape[0]
    row = lax.broadcasted_iota(I32, right_side.shape, 0)
    current = jnp.zeros(right_side.shape, F32)
    for t in range(tiles):
        turned = inverse_ref[t]
        if turned_ref is not None:
            turned = turned.T
            turned_ref[t] = turned
        current = jnp.where(
            row == t, lax.dot(right_side, turned, preferred_element_type=F32), current
        )
    return current.astype(BF16)


def step_kernel(
    step, coef_ref, parts_ref, base_ref, inverse_ref, tail_ref, cur_ref, ret_ref, pick_ref,
    cur_out, send_ref, ret_out=None, turned_ref=None,
):
    current = solve(parts_ref, base_ref, inverse_ref, turned_ref)
    tiles = current.shape[0]
    wide = current.astype(F32)
    retarded = wide * (1.0 + coef_ref[0:1, :]) + tail_ref[step]
    for back in range(1, step + 1):
        past = cur_ref[pl.ds((back - 1) * tiles, tiles), :]
        retarded = retarded + coef_ref[back : back + 1, :] * past.astype(F32)
    kept = cur_ref.shape[0] - tiles
    cur_out[...] = jnp.concatenate([current, cur_ref[:kept, :]], axis=0)
    history = jnp.concatenate([retarded.astype(BF16), ret_ref[:kept, :]], axis=0)
    if ret_out is not None:
        ret_out[...] = history
    send_ref[...] = lax.dot(
        pick_ref[...], halves_stacked(history), preferred_element_type=F32
    ).astype(BF16)


def last_kernel(coef_ref, parts_ref, base_ref, inverse_ref, cur_ref, state_ref, cur_out, state_out):
    current = solve(parts_ref, base_ref, inverse_ref)
    tiles = current.shape[0]
    past = [cur_ref[pl.ds((STEPS - 2 - n) * tiles, tiles), :] for n in range(STEPS - 1)] + [current]
    for n in range(STEPS):
        cur_out[n] = past[n]
    wide = [c.astype(F32) for c in past]
    for p in range(state_ref.shape[0]):
        pole = coef_ref[8 + p : 9 + p, :]
        state = state_ref[p]
        for n in range(STEPS):
            state = pole * state + wide[n]
        state_out[p] = state


def in_hbm(x):
    return pltpu.with_memory_space_constraint(x, pltpu.HBM)


def call(kernel, name, outs, specs, scratch=()):
    return pl.pallas_call(
        kernel,
        name=name,
        out_shape=outs,
        in_specs=specs,
        out_specs=jax.tree.map(lambda _: VMEM, outs),
        scratch_shapes=scratch,
        compiler_params=pltpu.CompilerParams(vmem_limit_bytes=8 << 20),
    )


def body(
    excitation,
    cur_hist,
    ret_hist,
    pole_state,
    self_inverse,
    near_mats,
    far_mats,
    poles,
    residues,
    near_src,
    near_delay,
    far_dest,
    far_delay,
    far_reader,
):
    groups = far_reader.shape[1]
    cap = far_reader.shape[3]
    classes = far_reader.shape[4]
    tiles = excitation.shape[1]
    width = excitation.shape[2]
    owners = lax.axis_size("own")
    group_tiles = tiles * owners
    slots = groups * cap
    past = HIST * tiles
    shape = jax.ShapeDtypeStruct

    history = ret_hist.reshape(past, width)
    names = far_dest.shape[1]
    pick, outgoing = call(
        first_kernel,
        "first",
        (shape((2 * slots, 2 * past), BF16), shape((2 * slots, LANES), BF16)),
        [HBM] * 3,
        [
            pltpu.VMEM((names, tiles), I32),
            pltpu.VMEM((names, tiles), I32),
            pltpu.VMEM((past, width), BF16),
            pltpu.SemaphoreType.DMA((3,)),
        ],
    )(in_hbm(far_dest.T), in_hbm(far_delay.T), in_hbm(history))

    current = cur_hist.reshape(past, width)
    sources = near_src.shape[0] * near_src.shape[2]
    poles_count = poles.shape[0]
    reader_hits, split, near_pick, tail, coef, base, *turned = call(
        tables_kernel,
        "tables",
        (
            shape((group_tiles, classes * slots), BF16),
            shape((2 * slots, 2 * slots), BF16),
            shape((sources * tiles, past), BF16),
            shape((STEPS - 1, tiles, width), F32),
            shape((8 + poles_count, width), F32),
            shape((tiles, width), F32),
            *[shape((classes // FAR_PIECES, width, width), BF16)] * FAR_PIECES,
        ),
        [HBM] * 10,
        [
            pltpu.SMEM((poles_count,), F32),
            pltpu.SMEM((poles_count,), F32),
            pltpu.VMEM((cap, classes, groups), I32),
            pltpu.VMEM((sources, tiles), I32),
            pltpu.VMEM((sources, tiles), I32),
            pltpu.VMEM(pole_state.shape, F32),
            pltpu.VMEM(far_mats.shape, BF16),
            pltpu.VMEM((past, width), BF16),
            pltpu.VMEM(near_mats.shape, BF16),
            pltpu.VMEM(excitation.shape, BF16),
            pltpu.SemaphoreType.DMA((9 + FAR_PIECES,)),
        ],
    )(
        in_hbm(poles),
        in_hbm(residues),
        in_hbm(far_reader[0, :, 0].transpose(1, 2, 0)),
        in_hbm(near_src.transpose(0, 2, 1).reshape(sources, tiles)),
        in_hbm(near_delay.transpose(0, 2, 1).reshape(sources, tiles)),
        in_hbm(pole_state),
        in_hbm(far_mats),
        in_hbm(current),
        in_hbm(near_mats),
        in_hbm(excitation),
    )

    inverse = self_inverse
    retarded = history
    for step in range(STEPS):
        incoming = lax.all_to_all(
            outgoing.reshape(groups, 2 * cap, LANES), "grp", split_axis=0, concat_axis=0, tiled=True
        ).reshape(2 * slots, LANES)
        if step == 0:
            incoming, tail, coef, base, reader_hits, near_pick, split, *turned = (
                lax.optimization_barrier(
                    (incoming, tail, coef, base, reader_hits, near_pick, split, *turned)
                )
            )
        sums = shape((group_tiles, width), BF16)
        terms = pltpu.VMEM((classes * slots, width), BF16)
        kept = (incoming, split, reader_hits, *turned)
        if step == 0:
            part = call(far_first_kernel, "far", sums, [VMEM] * len(kept), [terms])(*kept)
        else:
            part, base = call(
                functools.partial(far_kernel, step),
                "far",
                (sums, shape((tiles, width), F32)),
                [VMEM] * (len(kept) + 4),
                [terms],
            )(*kept, near_pick, current, near_mats, excitation)
        parts = lax.all_to_all(
            part.reshape(owners, tiles, width), "own", split_axis=0, concat_axis=0, tiled=True
        )
        if step + 1 < STEPS:
            outs = (shape((past, width), BF16), shape((2 * slots, LANES), BF16))
            if step + 2 < STEPS:
                outs = outs + (shape((past, width), BF16),)
            if step == 0:
                outs = outs + (shape(self_inverse.shape, BF16),)
            made = call(functools.partial(step_kernel, step), "step", outs, [VMEM] * 8)(
                coef, parts, base, inverse, tail, current, retarded, pick
            )
            current, outgoing = made[:2]
            if step + 2 < STEPS:
                retarded = made[2]
            if step == 0:
                inverse = made[3]
    return call(
        last_kernel,
        "last",
        (shape((STEPS, tiles, width), BF16), shape(pole_state.shape, F32)),
        [VMEM] * 6,
    )(coef, parts, base, inverse, current, pole_state)


def solution(mesh):
    in_specs = (
        P(None, ("grp", "own"), None),
        P(None, ("grp", "own"), None),
        P(None, ("grp", "own"), None),
        P(None, ("grp", "own"), None),
        P(("grp", "own"), None, None),
        P(),
        P(),
        P(),
        P(),
        P(None, ("grp", "own"), None),
        P(None, ("grp", "own"), None),
        P(("grp", "own"), None),
        P(("grp", "own"), None),
        P("grp", None, "own", None, None),
    )
    out_specs = (P(None, ("grp", "own"), None), P(None, ("grp", "own"), None))
    return jax.shard_map(body, mesh=mesh, in_specs=in_specs, out_specs=out_specs, check_vma=False)
```

```python
import functools

import jax
import jax.numpy as jnp
from jax import lax
from jax.experimental import pallas as pl
from jax.experimental.pallas import tpu as pltpu
from jax.sharding import PartitionSpec as P

STEPS = 4
HIST = 4
F32 = jnp.float32
BF16 = jnp.bfloat16
I32 = jnp.int32
LANES = 128
FAR_PIECES = 4
CONTRACT_LAST = (((1,), (1,)), ((), ()))
VMEM = pl.BlockSpec(memory_space=pltpu.VMEM)
HBM = pl.BlockSpec(memory_space=pltpu.HBM)


def halves_stacked(rows):
    return jnp.concatenate([rows[:, :LANES], rows[:, LANES:]], axis=0)


def shifted(x, bits):
    return lax.shift_right_logical(x, jnp.full(x.shape, bits, x.dtype))


def fetch(sem, *pairs):
    copies = [pltpu.make_async_copy(src, dst, sem.at[n]) for n, (src, dst) in enumerate(pairs)]
    for copy in copies:
        copy.start()
    return copies


def first_kernel(
    dest_hbm, delay_hbm, ret_hbm, pick_ref, out_ref, dest_ref, delay_ref, ret_ref, sem
):
    copies = fetch(sem, (dest_hbm, dest_ref), (delay_hbm, delay_ref), (ret_hbm, ret_ref))
    names, tiles = dest_ref.shape
    shape = pick_ref.shape
    rows, cols = shape
    at = lax.broadcasted_iota(I32, shape, 0)
    col = lax.broadcasted_iota(I32, (1, cols), 1)
    tile_bits = tiles.bit_length() - 1
    group = shifted(at, 2)
    slab = shifted(col, tile_bits)
    col_delay = (slab & (HIST - 1)) + 1
    col_half = shifted(col, tile_bits + HIST.bit_length() - 1)
    spread = jnp.where(
        lax.broadcasted_iota(I32, (tiles, cols), 0) == (col & (tiles - 1)), 1.0, 0.0
    ).astype(BF16)
    of = lax.broadcasted_iota(I32, (cols, cols), 0)
    earlier = jnp.where((shifted(of, tile_bits) == slab) & (of < col), 1.0, 0.0).astype(BF16)
    placed = (col_half == (shifted(at, 1) & 1)).astype(F32)
    rank = (at & 1).astype(F32)
    copies[0].wait()
    copies[1].wait()
    dest = lax.dot(dest_ref[...].astype(F32).astype(BF16), spread, preferred_element_type=F32)
    delay = lax.dot(delay_ref[...].astype(F32).astype(BF16), spread, preferred_element_type=F32)
    dest = dest.astype(I32)
    on_time = delay.astype(I32) == col_delay
    dest_on_time = jnp.where(on_time, dest, -1)
    named = jnp.zeros(shape, F32)
    timed = jnp.zeros(shape, F32)
    for j in range(names):
        named = jnp.where(dest[j : j + 1] == group, 1.0, named)
        timed = jnp.where(dest_on_time[j : j + 1] == group, placed, timed)
    before = lax.dot(named.astype(BF16), earlier, preferred_element_type=F32)
    pick = jnp.where(before == rank, timed, 0.0).astype(BF16)
    pick_ref[...] = pick
    copies[2].wait()
    out_ref[...] = lax.dot(
        pick, halves_stacked(ret_ref[...]), preferred_element_type=F32
    ).astype(BF16)


def tables_kernel(
    pole_hbm, residue_hbm, reader_hbm, src_hbm, delay_hbm, state_hbm, far_hbm,
    cur_hbm, near_hbm, exc_hbm, hits_ref, split_ref, near_pick_ref, tail_ref, coef_ref, base_ref,
    *rest,
):
    turned = rest[:FAR_PIECES]
    pole_ref, residue_ref, reader_ref, src_ref, delay_ref, state_ref = rest[FAR_PIECES:][:6]
    far_ref, cur_ref, near_ref, exc_ref, sem = rest[FAR_PIECES + 6 :]
    size = far_ref.shape[0] // FAR_PIECES
    copies = fetch(
        sem,
        (reader_hbm, reader_ref),
        (src_hbm, src_ref),
        (delay_hbm, delay_ref),
        (pole_hbm, pole_ref),
        (residue_hbm, residue_ref),
        (state_hbm, state_ref),
        (cur_hbm, cur_ref),
        (near_hbm, near_ref),
        (exc_hbm, exc_ref),
        *(
            (far_hbm.at[pl.ds(n * size, size)], far_ref.at[pl.ds(n * size, size)])
            for n in range(FAR_PIECES)
        ),
    )
    reader_copy, src_copy, delay_copy, pole_copy, residue_copy, state_copy = copies[:6]
    cap, classes, groups = reader_ref.shape
    slots = cap * groups
    group_tiles = hits_ref.shape[0]
    slot = lax.broadcasted_iota(I32, (slots, 1), 0)
    row = lax.broadcasted_iota(I32, (slots, 2 * slots), 1)
    group_bits = groups.bit_length() - 1
    start = 4 * (slot & (groups - 1)) + shifted(slot, group_bits)
    for h in range(2):
        split_ref[h * slots : (h + 1) * slots, :] = jnp.where(
            row == start + 2 * h, 1.0, 0.0
        ).astype(BF16)
    reader_copy.wait()
    readers = jnp.concatenate([reader_ref[c] for c in range(cap)], axis=1)
    place = lax.broadcasted_iota(I32, (group_tiles, slots), 0)
    for k in range(classes):
        hits_ref[:, k * slots : (k + 1) * slots] = jnp.where(
            place == readers[k : k + 1], 1.0, 0.0
        ).astype(BF16)
    src_copy.wait()
    delay_copy.wait()
    sources, tiles = src_ref.shape
    near_row = ((delay_ref[...] - 1) * tiles + src_ref[...]).astype(F32).astype(BF16)
    eye = jnp.where(
        lax.broadcasted_iota(I32, (tiles, tiles), 0) == lax.broadcasted_iota(I32, (tiles, tiles), 1),
        1.0,
        0.0,
    ).astype(BF16)
    near_col = lax.dot_general(eye, near_row, CONTRACT_LAST, preferred_element_type=F32)
    near_col = near_col.astype(I32)
    at = lax.broadcasted_iota(I32, (tiles, near_pick_ref.shape[1]), 1)
    near_pick_ref[...] = jnp.concatenate(
        [jnp.where(at == near_col[:, a : a + 1], 1.0, 0.0) for a in range(sources)], axis=0
    ).astype(BF16)
    pole_copy.wait()
    residue_copy.wait()
    state_copy.wait()
    count = state_ref.shape[0]
    scale = [residue_ref[p] for p in range(count)]
    width = coef_ref.shape[1]
    for n in range(STEPS):
        total = scale[0]
        for p in range(1, count):
            total = total + scale[p]
        coef_ref[n : n + 1, :] = jnp.full((1, width), total, F32)
        if n + 1 < STEPS:
            scale = [scale[p] * pole_ref[p] for p in range(count)]
            tail = scale[0] * state_ref[0]
            for p in range(1, count):
                tail = tail + scale[p] * state_ref[p]
            tail_ref[n] = tail
    for p in range(count):
        coef_ref[8 + p : 9 + p, :] = jnp.full((1, width), pole_ref[p], F32)
    for n in range(6, 9):
        copies[n].wait()
    base_ref[...] = near_base(0, near_pick_ref, cur_ref, near_ref, exc_ref)
    for n in range(FAR_PIECES):
        copies[9 + n].wait()
        for k in range(size):
            turned[n][k] = far_ref[n * size + k].T


def far_terms(entries, turned, terms_ref):
    slots = entries.shape[0]
    at = 0
    for piece in turned:
        for k in range(piece.shape[0]):
            terms = lax.dot(entries, piece[k], preferred_element_type=F32)
            terms_ref[pl.ds(at, slots), :] = terms.astype(BF16)
            at += slots


def entries_of(in_ref, split_ref):
    halves = lax.dot(split_ref[...], in_ref[...], preferred_element_type=F32).astype(BF16)
    slots = halves.shape[0] // 2
    return jnp.concatenate([halves[:slots], halves[slots:]], axis=1)


def near_base(step, near_pick_ref, cur_ref, near_ref, exc_ref):
    near_rows = lax.dot(near_pick_ref[...], cur_ref[...], preferred_element_type=F32).astype(BF16)
    classes = near_ref.shape[0]
    tiles = exc_ref.shape[1]
    per_class = near_rows.shape[0] // classes
    base = exc_ref[step].astype(F32)
    for k in range(classes):
        near = lax.dot_general(
            near_rows[k * per_class : (k + 1) * per_class],
            near_ref[k],
            CONTRACT_LAST,
            preferred_element_type=F32,
        )
        for m in range(per_class // tiles):
            base = base - near[m * tiles : (m + 1) * tiles]
    return base


def far_first_kernel(in_ref, split_ref, hits_ref, *rest):
    *turned, part_ref, terms_ref = rest
    far_terms(entries_of(in_ref, split_ref), turned, terms_ref)
    part_ref[...] = lax.dot(
        hits_ref[...], terms_ref[...], preferred_element_type=F32
    ).astype(BF16)


def far_kernel(step, in_ref, split_ref, hits_ref, *rest):
    *turned, near_pick_ref, cur_ref, near_ref, exc_ref, part_ref, base_ref, terms_ref = rest
    entries = entries_of(in_ref, split_ref)
    base_ref[...] = near_base(step, near_pick_ref, cur_ref, near_ref, exc_ref)
    far_terms(entries, turned, terms_ref)
    part_ref[...] = lax.dot(
        hits_ref[...], terms_ref[...], preferred_element_type=F32
    ).astype(BF16)


def solve(parts_ref, base_ref, inverse_ref, turned_ref=None):
    far_field = parts_ref[0].astype(F32)
    for o in range(1, parts_ref.shape[0]):
        far_field = far_field + parts_ref[o].astype(F32)
    right_side = (base_ref[...] - far_field).astype(BF16)
    tiles = right_side.shape[0]
    row = lax.broadcasted_iota(I32, right_side.shape, 0)
    current = jnp.zeros(right_side.shape, F32)
    for t in range(tiles):
        turned = inverse_ref[t]
        if turned_ref is not None:
            turned = turned.T
            turned_ref[t] = turned
        if turned_ref is not None and t % 2 == 0:
            product = lax.dot_general(
                right_side, inverse_ref[t], CONTRACT_LAST, preferred_element_type=F32
            )
        else:
            product = lax.dot(right_side, turned, preferred_element_type=F32)
        current = jnp.where(row == t, product, current)
    return current.astype(BF16)


def step_kernel(
    step, coef_ref, parts_ref, base_ref, inverse_ref, tail_ref, cur_ref, ret_ref, pick_ref,
    cur_out, send_ref, ret_out=None, turned_ref=None,
):
    current = solve(parts_ref, base_ref, inverse_ref, turned_ref)
    tiles = current.shape[0]
    wide = current.astype(F32)
    retarded = wide * (1.0 + coef_ref[0:1, :]) + tail_ref[step]
    for back in range(1, step + 1):
        past = cur_ref[pl.ds((back - 1) * tiles, tiles), :]
        retarded = retarded + coef_ref[back : back + 1, :] * past.astype(F32)
    kept = cur_ref.shape[0] - tiles
    cur_out[...] = jnp.concatenate([current, cur_ref[:kept, :]], axis=0)
    history = jnp.concatenate([retarded.astype(BF16), ret_ref[:kept, :]], axis=0)
    if ret_out is not None:
        ret_out[...] = history
    send_ref[...] = lax.dot(
        pick_ref[...], halves_stacked(history), preferred_element_type=F32
    ).astype(BF16)


def last_kernel(coef_ref, parts_ref, base_ref, inverse_ref, cur_ref, state_ref, cur_out, state_out):
    current = solve(parts_ref, base_ref, inverse_ref)
    tiles = current.shape[0]
    past = [cur_ref[pl.ds((STEPS - 2 - n) * tiles, tiles), :] for n in range(STEPS - 1)] + [current]
    for n in range(STEPS):
        cur_out[n] = past[n]
    wide = [c.astype(F32) for c in past]
    for p in range(state_ref.shape[0]):
        pole = coef_ref[8 + p : 9 + p, :]
        state = state_ref[p]
        for n in range(STEPS):
            state = pole * state + wide[n]
        state_out[p] = state


def in_hbm(x):
    return pltpu.with_memory_space_constraint(x, pltpu.HBM)


def call(kernel, name, outs, specs, scratch=()):
    return pl.pallas_call(
        kernel,
        name=name,
        out_shape=outs,
        in_specs=specs,
        out_specs=jax.tree.map(lambda _: VMEM, outs),
        scratch_shapes=scratch,
        compiler_params=pltpu.CompilerParams(vmem_limit_bytes=8 << 20),
    )


def body(
    excitation,
    cur_hist,
    ret_hist,
    pole_state,
    self_inverse,
    near_mats,
    far_mats,
    poles,
    residues,
    near_src,
    near_delay,
    far_dest,
    far_delay,
    far_reader,
):
    groups = far_reader.shape[1]
    cap = far_reader.shape[3]
    classes = far_reader.shape[4]
    tiles = excitation.shape[1]
    width = excitation.shape[2]
    owners = lax.axis_size("own")
    group_tiles = tiles * owners
    slots = groups * cap
    past = HIST * tiles
    shape = jax.ShapeDtypeStruct

    history = ret_hist.reshape(past, width)
    names = far_dest.shape[1]
    pick, outgoing = call(
        first_kernel,
        "first",
        (shape((2 * slots, 2 * past), BF16), shape((2 * slots, LANES), BF16)),
        [HBM] * 3,
        [
            pltpu.VMEM((names, tiles), I32),
            pltpu.VMEM((names, tiles), I32),
            pltpu.VMEM((past, width), BF16),
            pltpu.SemaphoreType.DMA((3,)),
        ],
    )(in_hbm(far_dest.T), in_hbm(far_delay.T), in_hbm(history))

    current = cur_hist.reshape(past, width)
    sources = near_src.shape[0] * near_src.shape[2]
    poles_count = poles.shape[0]
    reader_hits, split, near_pick, tail, coef, base, *turned = call(
        tables_kernel,
        "tables",
        (
            shape((group_tiles, classes * slots), BF16),
            shape((2 * slots, 2 * slots), BF16),
            shape((sources * tiles, past), BF16),
            shape((STEPS - 1, tiles, width), F32),
            shape((8 + poles_count, width), F32),
            shape((tiles, width), F32),
            *[shape((classes // FAR_PIECES, width, width), BF16)] * FAR_PIECES,
        ),
        [HBM] * 10,
        [
            pltpu.SMEM((poles_count,), F32),
            pltpu.SMEM((poles_count,), F32),
            pltpu.VMEM((cap, classes, groups), I32),
            pltpu.VMEM((sources, tiles), I32),
            pltpu.VMEM((sources, tiles), I32),
            pltpu.VMEM(pole_state.shape, F32),
            pltpu.VMEM(far_mats.shape, BF16),
            pltpu.VMEM((past, width), BF16),
            pltpu.VMEM(near_mats.shape, BF16),
            pltpu.VMEM(excitation.shape, BF16),
            pltpu.SemaphoreType.DMA((9 + FAR_PIECES,)),
        ],
    )(
        in_hbm(poles),
        in_hbm(residues),
        in_hbm(far_reader[0, :, 0].transpose(1, 2, 0)),
        in_hbm(near_src.transpose(0, 2, 1).reshape(sources, tiles)),
        in_hbm(near_delay.transpose(0, 2, 1).reshape(sources, tiles)),
        in_hbm(pole_state),
        in_hbm(far_mats),
        in_hbm(current),
        in_hbm(near_mats),
        in_hbm(excitation),
    )

    inverse = self_inverse
    retarded = history
    for step in range(STEPS):
        incoming = lax.all_to_all(
            outgoing.reshape(groups, 2 * cap, LANES), "grp", split_axis=0, concat_axis=0, tiled=True
        ).reshape(2 * slots, LANES)
        if step == 0:
            incoming, tail, coef, base, reader_hits, near_pick, split, *turned = (
                lax.optimization_barrier(
                    (incoming, tail, coef, base, reader_hits, near_pick, split, *turned)
                )
            )
        sums = shape((group_tiles, width), BF16)
        terms = pltpu.VMEM((classes * slots, width), BF16)
        kept = (incoming, split, reader_hits, *turned)
        if step == 0:
            part = call(far_first_kernel, "far", sums, [VMEM] * len(kept), [terms])(*kept)
        else:
            part, base = call(
                functools.partial(far_kernel, step),
                "far",
                (sums, shape((tiles, width), F32)),
                [VMEM] * (len(kept) + 4),
                [terms],
            )(*kept, near_pick, current, near_mats, excitation)
        parts = lax.all_to_all(
            part.reshape(owners, tiles, width), "own", split_axis=0, concat_axis=0, tiled=True
        )
        if step + 1 < STEPS:
            outs = (shape((past, width), BF16), shape((2 * slots, LANES), BF16))
            if step + 2 < STEPS:
                outs = outs + (shape((past, width), BF16),)
            if step == 0:
                outs = outs + (shape(self_inverse.shape, BF16),)
            made = call(functools.partial(step_kernel, step), "step", outs, [VMEM] * 8)(
                coef, parts, base, inverse, tail, current, retarded, pick
            )
            current, outgoing = made[:2]
            if step + 2 < STEPS:
                retarded = made[2]
            if step == 0:
                inverse = made[3]
    return call(
        last_kernel,
        "last",
        (shape((STEPS, tiles, width), BF16), shape(pole_state.shape, F32)),
        [VMEM] * 6,
    )(coef, parts, base, inverse, current, pole_state)


def solution(mesh):
    in_specs = (
        P(None, ("grp", "own"), None),
        P(None, ("grp", "own"), None),
        P(None, ("grp", "own"), None),
        P(None, ("grp", "own"), None),
        P(("grp", "own"), None, None),
        P(),
        P(),
        P(),
        P(),
        P(None, ("grp", "own"), None),
        P(None, ("grp", "own"), None),
        P(("grp", "own"), None),
        P(("grp", "own"), None),
        P("grp", None, "own", None, None),
    )
    out_specs = (P(None, ("grp", "own"), None), P(None, ("grp", "own"), None))
    return jax.shard_map(body, mesh=mesh, in_specs=in_specs, out_specs=out_specs, check_vma=False)
```

```python
import functools

import jax
import jax.numpy as jnp
from jax import lax
from jax.experimental import pallas as pl
from jax.experimental.pallas import tpu as pltpu
from jax.sharding import PartitionSpec as P

STEPS = 4
HIST = 4
F32 = jnp.float32
BF16 = jnp.bfloat16
I32 = jnp.int32
LANES = 128
FAR_PIECES = 4
CONTRACT_LAST = (((1,), (1,)), ((), ()))
VMEM = pl.BlockSpec(memory_space=pltpu.VMEM)
HBM = pl.BlockSpec(memory_space=pltpu.HBM)


def halves_stacked(rows):
    return jnp.concatenate([rows[:, :LANES], rows[:, LANES:]], axis=0)


def shifted(x, bits):
    return lax.shift_right_logical(x, jnp.full(x.shape, bits, x.dtype))


def fetch(sem, *pairs):
    copies = [pltpu.make_async_copy(src, dst, sem.at[n]) for n, (src, dst) in enumerate(pairs)]
    for copy in copies:
        copy.start()
    return copies


def first_kernel(
    dest_hbm, delay_hbm, ret_hbm, pick_ref, out_ref, dest_ref, delay_ref, ret_ref, sem
):
    copies = fetch(sem, (dest_hbm, dest_ref), (delay_hbm, delay_ref), (ret_hbm, ret_ref))
    names, tiles = dest_ref.shape
    shape = pick_ref.shape
    rows, cols = shape
    at = lax.broadcasted_iota(I32, shape, 0)
    col = lax.broadcasted_iota(I32, (1, cols), 1)
    tile_bits = tiles.bit_length() - 1
    group = shifted(at, 2)
    slab = shifted(col, tile_bits)
    col_delay = (slab & (HIST - 1)) + 1
    col_half = shifted(col, tile_bits + HIST.bit_length() - 1)
    spread = jnp.where(
        lax.broadcasted_iota(I32, (tiles, cols), 0) == (col & (tiles - 1)), 1.0, 0.0
    ).astype(BF16)
    of = lax.broadcasted_iota(I32, (cols, cols), 0)
    earlier = jnp.where((shifted(of, tile_bits) == slab) & (of < col), 1.0, 0.0).astype(BF16)
    placed = (col_half == (shifted(at, 1) & 1)).astype(F32)
    rank = (at & 1).astype(F32)
    copies[0].wait()
    copies[1].wait()
    dest = lax.dot(dest_ref[...].astype(F32).astype(BF16), spread, preferred_element_type=F32)
    delay = lax.dot(delay_ref[...].astype(F32).astype(BF16), spread, preferred_element_type=F32)
    dest = dest.astype(I32)
    on_time = delay.astype(I32) == col_delay
    dest_on_time = jnp.where(on_time, dest, -1)
    named = jnp.zeros(shape, F32)
    timed = jnp.zeros(shape, F32)
    for j in range(names):
        named = jnp.where(dest[j : j + 1] == group, 1.0, named)
        timed = jnp.where(dest_on_time[j : j + 1] == group, placed, timed)
    before = lax.dot(named.astype(BF16), earlier, preferred_element_type=F32)
    pick = jnp.where(before == rank, timed, 0.0).astype(BF16)
    pick_ref[...] = pick
    copies[2].wait()
    out_ref[...] = lax.dot(
        pick, halves_stacked(ret_ref[...]), preferred_element_type=F32
    ).astype(BF16)


def tables_kernel(
    pole_hbm, residue_hbm, reader_hbm, src_hbm, delay_hbm, state_hbm, far_hbm,
    cur_hbm, near_hbm, exc_hbm, hits_ref, split_ref, near_pick_ref, tail_ref, coef_ref, base_ref,
    *rest,
):
    turned = rest[:FAR_PIECES]
    pole_ref, residue_ref, reader_ref, src_ref, delay_ref, state_ref = rest[FAR_PIECES:][:6]
    far_ref, cur_ref, near_ref, exc_ref, sem = rest[FAR_PIECES + 6 :]
    size = far_ref.shape[0] // FAR_PIECES
    copies = fetch(
        sem,
        (reader_hbm, reader_ref),
        (src_hbm, src_ref),
        (delay_hbm, delay_ref),
        (pole_hbm, pole_ref),
        (residue_hbm, residue_ref),
        (state_hbm, state_ref),
        (cur_hbm, cur_ref),
        (near_hbm, near_ref),
        (exc_hbm, exc_ref),
        *(
            (far_hbm.at[pl.ds(n * size, size)], far_ref.at[pl.ds(n * size, size)])
            for n in range(FAR_PIECES)
        ),
    )
    reader_copy, src_copy, delay_copy, pole_copy, residue_copy, state_copy = copies[:6]
    cap, classes, groups = reader_ref.shape
    slots = cap * groups
    group_tiles = hits_ref.shape[0]
    slot = lax.broadcasted_iota(I32, (slots, 1), 0)
    row = lax.broadcasted_iota(I32, (slots, 2 * slots), 1)
    group_bits = groups.bit_length() - 1
    start = 4 * (slot & (groups - 1)) + shifted(slot, group_bits)
    for h in range(2):
        split_ref[h * slots : (h + 1) * slots, :] = jnp.where(
            row == start + 2 * h, 1.0, 0.0
        ).astype(BF16)
    reader_copy.wait()
    readers = jnp.concatenate([reader_ref[c] for c in range(cap)], axis=1)
    place = lax.broadcasted_iota(I32, (group_tiles, slots), 0)
    for k in range(classes):
        hits_ref[:, k * slots : (k + 1) * slots] = jnp.where(
            place == readers[k : k + 1], 1.0, 0.0
        ).astype(BF16)
    src_copy.wait()
    delay_copy.wait()
    sources, tiles = src_ref.shape
    near_row = ((delay_ref[...] - 1) * tiles + src_ref[...]).astype(F32).astype(BF16)
    eye = jnp.where(
        lax.broadcasted_iota(I32, (tiles, tiles), 0) == lax.broadcasted_iota(I32, (tiles, tiles), 1),
        1.0,
        0.0,
    ).astype(BF16)
    near_col = lax.dot_general(eye, near_row, CONTRACT_LAST, preferred_element_type=F32)
    near_col = near_col.astype(I32)
    at = lax.broadcasted_iota(I32, (tiles, near_pick_ref.shape[1]), 1)
    near_pick_ref[...] = jnp.concatenate(
        [jnp.where(at == near_col[:, a : a + 1], 1.0, 0.0) for a in range(sources)], axis=0
    ).astype(BF16)
    pole_copy.wait()
    residue_copy.wait()
    state_copy.wait()
    count = state_ref.shape[0]
    scale = [residue_ref[p] for p in range(count)]
    width = coef_ref.shape[1]
    for n in range(STEPS):
        total = scale[0]
        for p in range(1, count):
            total = total + scale[p]
        coef_ref[n : n + 1, :] = jnp.full((1, width), total, F32)
        if n + 1 < STEPS:
            scale = [scale[p] * pole_ref[p] for p in range(count)]
            tail = scale[0] * state_ref[0]
            for p in range(1, count):
                tail = tail + scale[p] * state_ref[p]
            tail_ref[n] = tail
    for p in range(count):
        coef_ref[8 + p : 9 + p, :] = jnp.full((1, width), pole_ref[p], F32)
    for n in range(6, 9):
        copies[n].wait()
    base_ref[...] = near_base(0, near_pick_ref, cur_ref, near_ref, exc_ref)
    for n in range(FAR_PIECES):
        copies[9 + n].wait()
        for k in range(size):
            turned[n][k] = far_ref[n * size + k].T


def far_terms(entries, turned, terms_ref):
    slots = entries.shape[0]
    at = 0
    for piece in turned:
        for k in range(piece.shape[0]):
            terms = lax.dot(entries, piece[k], preferred_element_type=F32)
            terms_ref[pl.ds(at, slots), :] = terms.astype(BF16)
            at += slots


def entries_of(in_ref, split_ref):
    halves = lax.dot(split_ref[...], in_ref[...], preferred_element_type=F32).astype(BF16)
    slots = halves.shape[0] // 2
    return jnp.concatenate([halves[:slots], halves[slots:]], axis=1)


def near_base(step, near_pick_ref, cur_ref, near_ref, exc_ref):
    near_rows = lax.dot(near_pick_ref[...], cur_ref[...], preferred_element_type=F32).astype(BF16)
    classes = near_ref.shape[0]
    tiles = exc_ref.shape[1]
    per_class = near_rows.shape[0] // classes
    base = exc_ref[step].astype(F32)
    for k in range(classes):
        near = lax.dot_general(
            near_rows[k * per_class : (k + 1) * per_class],
            near_ref[k],
            CONTRACT_LAST,
            preferred_element_type=F32,
        )
        for m in range(per_class // tiles):
            base = base - near[m * tiles : (m + 1) * tiles]
    return base


def far_first_kernel(in_ref, split_ref, hits_ref, *rest):
    *turned, part_ref, terms_ref = rest
    far_terms(entries_of(in_ref, split_ref), turned, terms_ref)
    part_ref[...] = lax.dot(
        hits_ref[...], terms_ref[...], preferred_element_type=F32
    ).astype(BF16)


def far_kernel(step, in_ref, split_ref, hits_ref, *rest):
    *turned, near_pick_ref, cur_ref, near_ref, exc_ref, part_ref, base_ref, terms_ref = rest
    entries = entries_of(in_ref, split_ref)
    base_ref[...] = near_base(step, near_pick_ref, cur_ref, near_ref, exc_ref)
    far_terms(entries, turned, terms_ref)
    part_ref[...] = lax.dot(
        hits_ref[...], terms_ref[...], preferred_element_type=F32
    ).astype(BF16)


def solve(parts_ref, base_ref, inverse_ref, turned_ref=None):
    far_field = parts_ref[0].astype(F32)
    for o in range(1, parts_ref.shape[0]):
        far_field = far_field + parts_ref[o].astype(F32)
    right_side = (base_ref[...] - far_field).astype(BF16)
    tiles = right_side.shape[0]
    row = lax.broadcasted_iota(I32, right_side.shape, 0)
    current = jnp.zeros(right_side.shape, F32)
    for t in range(tiles):
        turned = inverse_ref[t]
        if turned_ref is not None:
            turned = turned.T
            turned_ref[t] = turned
        if turned_ref is not None and t % 4 != 3:
            product = lax.dot_general(
                right_side, inverse_ref[t], CONTRACT_LAST, preferred_element_type=F32
            )
        else:
            product = lax.dot(right_side, turned, preferred_element_type=F32)
        current = jnp.where(row == t, product, current)
    return current.astype(BF16)


def step_kernel(
    step, coef_ref, parts_ref, base_ref, inverse_ref, tail_ref, cur_ref, ret_ref, pick_ref,
    cur_out, send_ref, ret_out=None, turned_ref=None,
):
    current = solve(parts_ref, base_ref, inverse_ref, turned_ref)
    tiles = current.shape[0]
    wide = current.astype(F32)
    retarded = wide * (1.0 + coef_ref[0:1, :]) + tail_ref[step]
    for back in range(1, step + 1):
        past = cur_ref[pl.ds((back - 1) * tiles, tiles), :]
        retarded = retarded + coef_ref[back : back + 1, :] * past.astype(F32)
    kept = cur_ref.shape[0] - tiles
    cur_out[...] = jnp.concatenate([current, cur_ref[:kept, :]], axis=0)
    history = jnp.concatenate([retarded.astype(BF16), ret_ref[:kept, :]], axis=0)
    if ret_out is not None:
        ret_out[...] = history
    send_ref[...] = lax.dot(
        pick_ref[...], halves_stacked(history), preferred_element_type=F32
    ).astype(BF16)


def last_kernel(coef_ref, parts_ref, base_ref, inverse_ref, cur_ref, state_ref, cur_out, state_out):
    current = solve(parts_ref, base_ref, inverse_ref)
    tiles = current.shape[0]
    past = [cur_ref[pl.ds((STEPS - 2 - n) * tiles, tiles), :] for n in range(STEPS - 1)] + [current]
    for n in range(STEPS):
        cur_out[n] = past[n]
    wide = [c.astype(F32) for c in past]
    for p in range(state_ref.shape[0]):
        pole = coef_ref[8 + p : 9 + p, :]
        state = state_ref[p]
        for n in range(STEPS):
            state = pole * state + wide[n]
        state_out[p] = state


def in_hbm(x):
    return pltpu.with_memory_space_constraint(x, pltpu.HBM)


def call(kernel, name, outs, specs, scratch=()):
    return pl.pallas_call(
        kernel,
        name=name,
        out_shape=outs,
        in_specs=specs,
        out_specs=jax.tree.map(lambda _: VMEM, outs),
        scratch_shapes=scratch,
        compiler_params=pltpu.CompilerParams(vmem_limit_bytes=8 << 20),
    )


def body(
    excitation,
    cur_hist,
    ret_hist,
    pole_state,
    self_inverse,
    near_mats,
    far_mats,
    poles,
    residues,
    near_src,
    near_delay,
    far_dest,
    far_delay,
    far_reader,
):
    groups = far_reader.shape[1]
    cap = far_reader.shape[3]
    classes = far_reader.shape[4]
    tiles = excitation.shape[1]
    width = excitation.shape[2]
    owners = lax.axis_size("own")
    group_tiles = tiles * owners
    slots = groups * cap
    past = HIST * tiles
    shape = jax.ShapeDtypeStruct

    history = ret_hist.reshape(past, width)
    names = far_dest.shape[1]
    pick, outgoing = call(
        first_kernel,
        "first",
        (shape((2 * slots, 2 * past), BF16), shape((2 * slots, LANES), BF16)),
        [HBM] * 3,
        [
            pltpu.VMEM((names, tiles), I32),
            pltpu.VMEM((names, tiles), I32),
            pltpu.VMEM((past, width), BF16),
            pltpu.SemaphoreType.DMA((3,)),
        ],
    )(in_hbm(far_dest.T), in_hbm(far_delay.T), in_hbm(history))

    current = cur_hist.reshape(past, width)
    sources = near_src.shape[0] * near_src.shape[2]
    poles_count = poles.shape[0]
    reader_hits, split, near_pick, tail, coef, base, *turned = call(
        tables_kernel,
        "tables",
        (
            shape((group_tiles, classes * slots), BF16),
            shape((2 * slots, 2 * slots), BF16),
            shape((sources * tiles, past), BF16),
            shape((STEPS - 1, tiles, width), F32),
            shape((8 + poles_count, width), F32),
            shape((tiles, width), F32),
            *[shape((classes // FAR_PIECES, width, width), BF16)] * FAR_PIECES,
        ),
        [HBM] * 10,
        [
            pltpu.SMEM((poles_count,), F32),
            pltpu.SMEM((poles_count,), F32),
            pltpu.VMEM((cap, classes, groups), I32),
            pltpu.VMEM((sources, tiles), I32),
            pltpu.VMEM((sources, tiles), I32),
            pltpu.VMEM(pole_state.shape, F32),
            pltpu.VMEM(far_mats.shape, BF16),
            pltpu.VMEM((past, width), BF16),
            pltpu.VMEM(near_mats.shape, BF16),
            pltpu.VMEM(excitation.shape, BF16),
            pltpu.SemaphoreType.DMA((9 + FAR_PIECES,)),
        ],
    )(
        in_hbm(poles),
        in_hbm(residues),
        in_hbm(far_reader[0, :, 0].transpose(1, 2, 0)),
        in_hbm(near_src.transpose(0, 2, 1).reshape(sources, tiles)),
        in_hbm(near_delay.transpose(0, 2, 1).reshape(sources, tiles)),
        in_hbm(pole_state),
        in_hbm(far_mats),
        in_hbm(current),
        in_hbm(near_mats),
        in_hbm(excitation),
    )

    inverse = self_inverse
    retarded = history
    for step in range(STEPS):
        incoming = lax.all_to_all(
            outgoing.reshape(groups, 2 * cap, LANES), "grp", split_axis=0, concat_axis=0, tiled=True
        ).reshape(2 * slots, LANES)
        if step == 0:
            incoming, tail, coef, base, reader_hits, near_pick, split, *turned = (
                lax.optimization_barrier(
                    (incoming, tail, coef, base, reader_hits, near_pick, split, *turned)
                )
            )
        sums = shape((group_tiles, width), BF16)
        terms = pltpu.VMEM((classes * slots, width), BF16)
        kept = (incoming, split, reader_hits, *turned)
        if step == 0:
            part = call(far_first_kernel, "far", sums, [VMEM] * len(kept), [terms])(*kept)
        else:
            part, base = call(
                functools.partial(far_kernel, step),
                "far",
                (sums, shape((tiles, width), F32)),
                [VMEM] * (len(kept) + 4),
                [terms],
            )(*kept, near_pick, current, near_mats, excitation)
        parts = lax.all_to_all(
            part.reshape(owners, tiles, width), "own", split_axis=0, concat_axis=0, tiled=True
        )
        if step + 1 < STEPS:
            outs = (shape((past, width), BF16), shape((2 * slots, LANES), BF16))
            if step + 2 < STEPS:
                outs = outs + (shape((past, width), BF16),)
            if step == 0:
                outs = outs + (shape(self_inverse.shape, BF16),)
            made = call(functools.partial(step_kernel, step), "step", outs, [VMEM] * 8)(
                coef, parts, base, inverse, tail, current, retarded, pick
            )
            current, outgoing = made[:2]
            if step + 2 < STEPS:
                retarded = made[2]
            if step == 0:
                inverse = made[3]
    return call(
        last_kernel,
        "last",
        (shape((STEPS, tiles, width), BF16), shape(pole_state.shape, F32)),
        [VMEM] * 6,
    )(coef, parts, base, inverse, current, pole_state)


def solution(mesh):
    in_specs = (
        P(None, ("grp", "own"), None),
        P(None, ("grp", "own"), None),
        P(None, ("grp", "own"), None),
        P(None, ("grp", "own"), None),
        P(("grp", "own"), None, None),
        P(),
        P(),
        P(),
        P(),
        P(None, ("grp", "own"), None),
        P(None, ("grp", "own"), None),
        P(("grp", "own"), None),
        P(("grp", "own"), None),
        P("grp", None, "own", None, None),
    )
    out_specs = (P(None, ("grp", "own"), None), P(None, ("grp", "own"), None))
    return jax.shard_map(body, mesh=mesh, in_specs=in_specs, out_specs=out_specs, check_vma=False)
```
